32 devices in a mesh: ctx: 8 (over z, y), fsdp: 4 (over x, core).
Axes of the slice: x: 2, y: 2, z: 4, core: 2. Of those that a mesh axis runs over, the one named last changes fastest.
Arguments:
- tokens: bfloat16 [4, 1024, 2048], P('fsdp', 'ctx'), may hold values from -6 to 6
- cotangent: bfloat16 [4, 1024, 2048], P('fsdp', 'ctx'), may hold values from -6 to 6
- pair_table: int32 [8], replicated, may hold values from 0 to 7, each once
- doc_lengths: int32 [4, 3], P('fsdp'), may hold values from 1 to 512, 1024 in all within a row
- attn_gain: bfloat16 [2048], P('fsdp'), may hold values from 0.099609375 to 1.8984375
- query_weight: bfloat16 [2048, 2048], P('fsdp'), may hold values from -0.125 to 0.125
- key_matrix: bfloat16 [2048, 512], P('fsdp'), may hold values from -0.125 to 0.125
- value_matrix: bfloat16 [2048, 512], P('fsdp'), may hold values from -0.125 to 0.125
- output_weight: bfloat16 [2048, 2048], P('fsdp'), may hold values from -1 to 1
- mlp_gain: bfloat16 [2048], P('fsdp'), may hold values from 0.099609375 to 1.8984375
- gate_weight: bfloat16 [2048, 8192], P('fsdp'), may hold values from -0.125 to 0.125
- up_weight: bfloat16 [2048, 8192], P('fsdp'), may hold values from -0.125 to 0.125
- down_weight: bfloat16 [8192, 2048], P('fsdp'), may hold values from -0.0625 to 0.0625
Outputs:
- output: bfloat16 [4, 1024, 2048], P('fsdp', 'ctx')
- input_grad: bfloat16 [4, 1024, 2048], P('fsdp', 'ctx')
- attn_gain_grad: float32 [2048], P(('ctx', 'fsdp'))
- query_weight_grad: float32 [2048, 2048], P(('ctx', 'fsdp'))
- key_weight_grad: float32 [2048, 512], P(('ctx', 'fsdp'))
- value_weight_grad: float32 [2048, 512], P(('ctx', 'fsdp'))
- output_weight_grad: float32 [2048, 2048], P(('ctx', 'fsdp'))
- mlp_gain_grad: float32 [2048], P(('ctx', 'fsdp'))
- gate_weight_grad: float32 [2048, 8192], P(('ctx', 'fsdp'))
- up_weight_grad: float32 [2048, 8192], P(('ctx', 'fsdp'))
- down_weight_grad: float32 [8192, 2048], P(('ctx', 'fsdp'))
The draws below stay inside these ranges and needn't reach their ends.
Inputs may be any that keep to these rules, and one draw needn't show every extreme that they name: `pair_table`: each index of ctx appears exactly once. `doc_lengths`: the 3 documents of a sequence fill its 1024 positions in order; in every sequence one document has exactly 512 positions.
All inputs are finite; a program needn't handle non-finite values.
Results may differ from the reference program's by a relative error of at most 0.017.
Values may be sent and summed in bfloat16 or wider, within the bound.
No kernel may reach another device: no remote copies, remote signals or barrier semaphores. Data moves between devices by JAX's collectives and lax.ppermute only.
A program may use at most 512 MiB of HBM per device.

```python
import math
import jax
import jax.numpy as jnp
import numpy as np
from jax import lax

MODEL_WIDTH = 2048
QUERY_HEADS = 32
KEY_VALUE_HEADS = 8
HEAD_SIZE = 64
FF = 8192
DOCS = 3
BLK = 64
LENGTH = 1024
SEQS = 4
N_CTX = 8


def levels(key, extent, shards, low, high):
    def one(axis_at, blocks):
        draws = jax.random.uniform(jax.random.fold_in(jax.random.fold_in(key, 6), axis_at), (blocks,), jnp.float32, low / len(shards), high / len(shards))
        return jnp.repeat(jnp.exp(draws), extent[axis_at] // blocks).reshape((-1,) + (1,) * (len(extent) - axis_at - 1))

    loudness = one(*shards[0])
    for cut in shards[1:]:
        loudness = loudness * one(*cut)
    return loudness


def profile(amount, total, reach, slope):
    weights = [(1 << 20) // math.isqrt(grade ** slope) + 1 for grade in range(2, amount + 1)]
    surplus, given = total - reach - (amount - 1), [1] * (amount - 1)
    while surplus > 0:
        free = [i for i in range(amount - 1) if given[i] < reach]
        pool, remaining = sum([weights[i] for i in free]), surplus
        for i in free:
            more = min(reach - given[i], max(1, remaining * weights[i] // pool), surplus)
            given[i] = given[i] + more
            surplus = surplus - more
    return np.array([reach] + given)


def ragged_sizes(rng, count, total, bound, lean):
    if count == 2:
        one = jax.random.randint(rng, (), max(1, total - bound), min(bound, total - 1) + 1)
        return jnp.stack([one, total - one])
    tallies = jnp.asarray(profile(count, total, bound, lean), jnp.int32)
    pairs = (count - 1) // 2
    donor, receiver = tallies[1:1 + 2 * pairs:2], tallies[2:2 + 2 * pairs:2]
    slack = jnp.minimum(donor - 1, bound - receiver)
    shifted = jax.random.randint(jax.random.fold_in(rng, 1), (pairs,), 0, 1 << 20) % (slack + 1)
    tallies = tallies.at[1:1 + 2 * pairs:2].set(donor - shifted).at[2:2 + 2 * pairs:2].set(receiver + shifted)
    return tallies[jax.random.permutation(jax.random.fold_in(rng, 2), count)]


def gaussian(key, shape, scale, reach, shards=(), kind=jnp.bfloat16):
    drawn = scale * jax.random.normal(key, shape, jnp.float32)
    if shards:
        drawn = drawn * levels(key, shape, shards, -0.22, 0.18)
    return jnp.clip(drawn, -reach, reach).astype(kind)


def setup_inputs(seed: int = 0) -> dict:
    seeds = jax.random.split(jax.random.key(seed), 14)
    tokens = gaussian(seeds[0], (SEQS, LENGTH, MODEL_WIDTH), 1.0, 6.0, ((0, 4), (1, 8)))
    cotangent = gaussian(seeds[1], (SEQS, LENGTH, MODEL_WIDTH), 1.0, 6.0, ((0, 4), (1, 8)))
    pair_table = jax.random.permutation(seeds[2], N_CTX).astype(jnp.int32)
    doc_lengths = jax.vmap(lambda own: ragged_sizes(own, DOCS, LENGTH, LENGTH // 2, 2))(jax.random.split(seeds[3], SEQS)).reshape((SEQS, DOCS)).astype(jnp.int32)
    attn_gain = jnp.clip(1.0 + 0.18 * jax.random.normal(seeds[4], (MODEL_WIDTH,), jnp.float32), 0.099609375, 1.8984375).astype(jnp.bfloat16)
    query_weight = gaussian(seeds[5], (MODEL_WIDTH, QUERY_HEADS * HEAD_SIZE), MODEL_WIDTH ** -0.5, 0.125, ((0, 4),))
    key_matrix = gaussian(seeds[6], (MODEL_WIDTH, KEY_VALUE_HEADS * HEAD_SIZE), MODEL_WIDTH ** -0.5, 0.125, ((0, 4),))
    value_matrix = gaussian(seeds[7], (MODEL_WIDTH, KEY_VALUE_HEADS * HEAD_SIZE), MODEL_WIDTH ** -0.5, 0.125, ((0, 4),))
    output_weight = gaussian(seeds[8], (QUERY_HEADS * HEAD_SIZE, MODEL_WIDTH), (QUERY_HEADS * HEAD_SIZE // 64) ** -0.5, 1.0, ((0, 4),))
    mlp_gain = jnp.clip(1.0 + 0.18 * jax.random.normal(seeds[9], (MODEL_WIDTH,), jnp.float32), 0.099609375, 1.8984375).astype(jnp.bfloat16)
    gate_weight = gaussian(seeds[10], (MODEL_WIDTH, FF), MODEL_WIDTH ** -0.5, 0.125, ((0, 4),))
    up_weight = gaussian(seeds[11], (MODEL_WIDTH, FF), MODEL_WIDTH ** -0.5, 0.125, ((0, 4),))
    down_weight = gaussian(seeds[12], (FF, MODEL_WIDTH), FF ** -0.5, 0.0625, ((0, 4),))
    return dict(tokens=tokens, cotangent=cotangent, pair_table=pair_table, doc_lengths=doc_lengths, attn_gain=attn_gain, query_weight=query_weight, key_matrix=key_matrix, value_matrix=value_matrix, output_weight=output_weight, mlp_gain=mlp_gain, gate_weight=gate_weight, up_weight=up_weight, down_weight=down_weight)


epsilon = 1e-05
masked_score = -1e+30
highest = lax.Precision.HIGHEST

@jax.custom_vjp
def reduced_precision(v):
    return lax.optimization_barrier(v.astype(jnp.bfloat16)).astype(jnp.float32)

@jax.custom_vjp
def reduced_backward(v):
    return v

def low_keep(v):
    return (reduced_precision(v), None)

def low_pass(kept, grad):
    return (grad,)

def back_keep(v):
    return (v, None)

def back_low(kept, grad):
    return (reduced_precision(grad),)
reduced_precision.defvjp(low_keep, low_pass)
reduced_backward.defvjp(back_keep, back_low)

def matrix_product(left_rows, right_side):
    return jnp.dot(left_rows, right_side, precision=highest, preferred_element_type=jnp.float32)

def rms_norm(values_in, norm_gain):
    scale_row = lax.rsqrt(lax.optimization_barrier(jnp.mean(values_in * values_in, axis=-1, keepdims=True)) + epsilon)
    return values_in * scale_row * norm_gain

def rope_tables(rot_places, half_dim):
    frequency = 1.0 / 500000.0 ** (jnp.arange(half_dim, dtype=jnp.float32) * 2.0 / (2 * half_dim))
    angles = rot_places.astype(jnp.float32)[..., None] * frequency
    return (jnp.cos(angles), jnp.sin(angles))

def apply_rotation(vectors, cosine_table, sine_table):
    half_dim = vectors.shape[-1] // 2
    front_half = vectors[..., :half_dim]
    back_half = vectors[..., half_dim:]
    cos_heads = cosine_table[..., None, :]
    sin_heads = sine_table[..., None, :]
    return jnp.concatenate([front_half * cos_heads - back_half * sin_heads, back_half * cos_heads + front_half * sin_heads], axis=-1)

def layout_places(pair_table, block_len, sequence_length):
    row_ids = jnp.arange(sequence_length, dtype=jnp.int32)
    shard_ids = row_ids // (2 * block_len)
    within = row_ids % (2 * block_len)
    num_devices = pair_table.shape[0]
    device_ids = jnp.arange(num_devices, dtype=jnp.int32)
    chosen = lax.optimization_barrier(jnp.sum(jnp.where(shard_ids[:, None] == device_ids[None, :], pair_table[None, :], 0), axis=1)).astype(jnp.int32)
    block_ids = jnp.where(within < block_len, chosen, 2 * num_devices - 1 - chosen)
    return (block_ids * block_len + within % block_len).astype(jnp.int32)

def document_places(places, lengths_row):
    doc_ends = jnp.cumsum(lengths_row).astype(jnp.int32)
    doc_starts = (doc_ends - lengths_row).astype(jnp.int32)
    doc_ids = lax.optimization_barrier(jnp.sum((places[:, None] >= doc_ends[None, :]).astype(jnp.int32), axis=1)).astype(jnp.int32)
    doc_numbers = jnp.arange(lengths_row.shape[0], dtype=jnp.int32)
    picked = lax.optimization_barrier(jnp.sum(jnp.where(doc_ids[:, None] == doc_numbers[None, :], doc_starts[None, :], 0), axis=1)).astype(jnp.int32)
    return (doc_ids, (places - picked).astype(jnp.int32))

def layer_sequence(params, seq_inputs, places, seq_docs, seq_rot):
    attn_gain, query_weight, key_matrix, value_matrix, output_weight, mlp_gain, gate_weight, up_weight, down_weight = params
    sequence_length = seq_inputs.shape[0]
    query_group_width = QUERY_HEADS // KEY_VALUE_HEADS
    score_scale = 1.0 / math.sqrt(HEAD_SIZE)
    first_normalized = reduced_precision(rms_norm(seq_inputs, attn_gain))
    queries = reduced_backward(matrix_product(first_normalized, query_weight))
    key_unrotated = reduced_backward(matrix_product(first_normalized, key_matrix))
    value_rows_reduced = reduced_precision(reduced_backward(matrix_product(first_normalized, value_matrix))).reshape(sequence_length, KEY_VALUE_HEADS, HEAD_SIZE)
    cosine_table, sine_table = rope_tables(seq_rot, HEAD_SIZE // 2)
    query_rotated_rows = reduced_precision(apply_rotation(queries.reshape(sequence_length, QUERY_HEADS, HEAD_SIZE), cosine_table, sine_table))
    key_rotated_rows = reduced_precision(apply_rotation(key_unrotated.reshape(sequence_length, KEY_VALUE_HEADS, HEAD_SIZE), cosine_table, sine_table))
    block_row_span = 2 * BLK
    query_block_list = query_rotated_rows.reshape(sequence_length // block_row_span, block_row_span, KEY_VALUE_HEADS, query_group_width, HEAD_SIZE)
    place_blocks = places.reshape(sequence_length // block_row_span, block_row_span)
    doc_blocks = seq_docs.reshape(sequence_length // block_row_span, block_row_span)

    def attend_block(operands):
        block_query, block_place, block_doc = operands
        scores = jnp.einsum('rkgd,lkd->kgrl', block_query, key_rotated_rows, precision=highest, preferred_element_type=jnp.float32) * score_scale
        scores = reduced_backward(scores)
        allowed = (places[None, :] <= block_place[:, None]) & (seq_docs[None, :] == block_doc[:, None])
        scores = jnp.where(allowed[None, None], scores, masked_score)
        row_max = lax.optimization_barrier(jnp.max(scores, axis=-1, keepdims=True))
        exponent = jnp.exp(scores - row_max)
        attn_probs = reduced_precision(exponent / lax.optimization_barrier(jnp.sum(exponent, axis=-1, keepdims=True)))
        return jnp.einsum('kgrl,lkd->rkgd', attn_probs, value_rows_reduced, precision=highest, preferred_element_type=jnp.float32)
    attn_mixed = lax.map(jax.checkpoint(attend_block), (query_block_list, place_blocks, doc_blocks))
    attn_mixed = reduced_precision(reduced_backward(attn_mixed.reshape(sequence_length, QUERY_HEADS * HEAD_SIZE)))
    hidden = seq_inputs + reduced_backward(matrix_product(attn_mixed, output_weight))
    normed_two = reduced_precision(rms_norm(hidden, mlp_gain))
    gate_proj = reduced_backward(matrix_product(normed_two, gate_weight))
    up_proj = reduced_backward(matrix_product(normed_two, up_weight))
    activated = reduced_precision(jax.nn.silu(gate_proj) * up_proj)
    return hidden + matrix_product(activated, down_weight)

def reference(tokens, cotangent, pair_table, doc_lengths, attn_gain, query_weight, key_matrix, value_matrix, output_weight, mlp_gain, gate_weight, up_weight, down_weight):
    places = layout_places(pair_table, BLK, LENGTH)
    row_docs, row_rot = jax.vmap(document_places, in_axes=(None, 0))(places, doc_lengths)
    params = (attn_gain.astype(jnp.float32), query_weight.astype(jnp.float32), key_matrix.astype(jnp.float32), value_matrix.astype(jnp.float32), output_weight.astype(jnp.float32), mlp_gain.astype(jnp.float32), gate_weight.astype(jnp.float32), up_weight.astype(jnp.float32), down_weight.astype(jnp.float32))

    def forward(all_inputs, all_params):

        def one_sequence(operands):
            seq_inputs, seq_docs, seq_rot = operands
            return layer_sequence(all_params, seq_inputs, places, seq_docs, seq_rot)
        return lax.map(jax.checkpoint(one_sequence), (all_inputs, row_docs, row_rot))
    outputs, pullback = jax.vjp(forward, tokens.astype(jnp.float32), params)
    grad_inputs, grad_params = pullback(cotangent.astype(jnp.float32))
    return (outputs.astype(jnp.bfloat16), grad_inputs.astype(jnp.bfloat16), grad_params[0], grad_params[1], grad_params[2], grad_params[3], grad_params[4], grad_params[5], grad_params[6], grad_params[7], grad_params[8])
```

```python
import math

import jax
import jax.numpy as jnp
from jax import lax
from jax.sharding import Mesh
from jax.sharding import PartitionSpec as P

MODEL_WIDTH = 2048
QUERY_HEADS = 32
KEY_VALUE_HEADS = 8
HEAD_SIZE = 64


epsilon = 1e-05
masked_score = -1e30


def rms_forward(values_in, norm_gain):
    scale_row = lax.rsqrt(jnp.mean(values_in * values_in, axis=-1, keepdims=True) + epsilon)
    return (values_in * scale_row * norm_gain, scale_row)


def rms_backward(values_in, scale_row, norm_gain, grad_normed):
    weighted = grad_normed * norm_gain
    inner_sum = jnp.mean(weighted * values_in, axis=-1, keepdims=True)
    grad_values = scale_row * weighted - values_in * scale_row * scale_row * scale_row * inner_sum
    grad_gain = jnp.sum(grad_normed * values_in * scale_row, axis=0)
    return (grad_values, grad_gain)


def rope_tables(rot_places, half_dim):
    frequency = 1.0 / 500000.0 ** (jnp.arange(half_dim, dtype=jnp.float32) * 2.0 / (2 * half_dim))
    angles = rot_places.astype(jnp.float32)[..., None] * frequency
    return (jnp.cos(angles), jnp.sin(angles))


def apply_rotation(vectors, cosine_table, sine_table):
    half_dim = vectors.shape[-1] // 2
    front_half = vectors[..., :half_dim]
    back_half = vectors[..., half_dim:]
    cos_heads = cosine_table[..., None, :]
    sin_heads = sine_table[..., None, :]
    return jnp.concatenate(
        [
            front_half * cos_heads - back_half * sin_heads,
            back_half * cos_heads + front_half * sin_heads,
        ],
        axis=-1,
    )


def inverse_rotation(vectors, cosine_table, sine_table):
    half_dim = vectors.shape[-1] // 2
    front_half = vectors[..., :half_dim]
    back_half = vectors[..., half_dim:]
    cos_heads = cosine_table[..., None, :]
    sin_heads = sine_table[..., None, :]
    return jnp.concatenate(
        [
            front_half * cos_heads + back_half * sin_heads,
            back_half * cos_heads - front_half * sin_heads,
        ],
        axis=-1,
    )


def layout_places(pair_table, block_len, sequence_length):
    row_ids = jnp.arange(sequence_length, dtype=jnp.int32)
    shard_ids = row_ids // (2 * block_len)
    within = row_ids % (2 * block_len)
    num_devices = pair_table.shape[0]
    device_ids = jnp.arange(num_devices, dtype=jnp.int32)
    chosen = jnp.sum(
        jnp.where(shard_ids[:, None] == device_ids[None, :], pair_table[None, :], 0), axis=1
    )
    block_ids = jnp.where(within < block_len, chosen, 2 * num_devices - 1 - chosen)
    return block_ids * block_len + within % block_len


def document_places(places, lengths_row):
    doc_ends = jnp.cumsum(lengths_row)
    doc_starts = doc_ends - lengths_row
    doc_ids = jnp.sum((places[:, None] >= doc_ends[None, :]).astype(jnp.int32), axis=1)
    doc_numbers = jnp.arange(lengths_row.shape[0], dtype=jnp.int32)
    picked = jnp.sum(
        jnp.where(doc_ids[:, None] == doc_numbers[None, :], doc_starts[None, :], 0), axis=1
    )
    return (doc_ids, places - picked)


EVERY = ("c", "x", "k")
CHIPS = ("c", "x")


class Wires:
    def __init__(self, ctx_count):
        self.count = ctx_count
        self.total = ctx_count * 4
        self.paths = ctx_count == 8
        self.c = lax.axis_index("c")
        self.x = lax.axis_index("x")
        self.k = lax.axis_index("k")
        self.f = 2 * self.x + self.k
        if self.paths:
            z_of = lambda i: i >> 3
            middle = [i for i in range(32) if z_of(i) in (1, 2)]
            ends = [i for i in range(32) if z_of(i) in (0, 3)]
            self.mid = [(i, i ^ 24) for i in middle]
            self.outward = [(i, i ^ 8) for i in middle]
            self.inward = [(i, i ^ 8) for i in ends]
            z_index = self.c // 2
            self.inner = (z_index == 1) | (z_index == 2)

    def swap(self, value, bits):
        return lax.ppermute(value, EVERY, [(i, i ^ bits) for i in range(self.total)])

    def send(self, value, pairs):
        return lax.ppermute(value, EVERY, pairs)

    def over_fsdp(self, shard):
        other = self.swap(shard, 2)
        near = self.x == 0
        both = jnp.stack([jnp.where(near, shard, other), jnp.where(near, other, shard)])
        partner = self.swap(both, 1)
        first = self.k == 0
        even = jnp.where(first, both, partner)
        odd = jnp.where(first, partner, both)
        return jnp.stack([even, odd], axis=1).reshape((-1,) + shard.shape[1:])

    def sum_fsdp(self, parts, axis):
        grid = jnp.moveaxis(parts, axis, 0)
        grid = grid.reshape((2, 2) + grid.shape[1:])
        mine = lax.dynamic_index_in_dim(grid, self.k, 1, keepdims=False)
        theirs = lax.dynamic_index_in_dim(grid, 1 - self.k, 1, keepdims=False)
        pair_sum = mine + self.swap(theirs, 1)
        mine = lax.dynamic_index_in_dim(pair_sum, self.x, 0, keepdims=False)
        theirs = lax.dynamic_index_in_dim(pair_sum, 1 - self.x, 0, keepdims=False)
        return mine + self.swap(theirs, 2)

    def ctx_gather(self, value):
        return lax.all_gather(value, "c", axis=0, tiled=False)

    def z_spread(self, value):
        step = self.swap(value, 8)
        over = self.send(value, self.mid)
        over_step = self.send(step, self.mid)
        out = self.send(over, self.outward)
        out_step = self.send(over_step, self.outward)
        second = jnp.where(self.inner, over_step, out)
        third = jnp.where(self.inner, over, out_step)
        return jnp.stack([value, step, second, third])

    def z_collect(self, parts):
        own, near, far, across = parts[0], parts[1], parts[2], parts[3]
        low = jnp.bfloat16
        wide = jnp.float32
        got = self.send(jnp.stack([far, across]).astype(low), self.inward).astype(wide)
        across = across + got[0]
        far = far + got[1]
        got = self.send(jnp.stack([across, far]).astype(low), self.mid).astype(wide)
        own = own + got[0]
        near = near + got[1]
        return own + self.swap(near.astype(low), 8).astype(wide)

    def spread(self, value):
        if not self.paths:
            return [lax.all_gather(value, CHIPS, axis=0, tiled=True)]
        half = value.shape[0] // 2
        width = value.shape[1]
        found = []
        for rows, order in ((value[:half], (4, 2)), (value[half:], (2, 4))):
            held = self.z_spread(rows)
            for bits in order:
                held = jnp.stack([held, self.swap(held, bits)])
            found.append(held.reshape(16 * half, width))
        return found

    def collect(self, parts):
        if not self.paths:
            low = parts[0].astype(jnp.bfloat16)
            return lax.psum_scatter(low, CHIPS, scatter_dimension=0, tiled=True).astype(jnp.float32)
        found = []
        for part, order in zip(parts, ((2, 4), (4, 2))):
            half = part.shape[0] // 16
            held = part.reshape(2, 2, 4, half, part.shape[1])
            for bits in order:
                held = held[0] + self.swap(held[1].astype(jnp.bfloat16), bits).astype(jnp.float32)
            found.append(self.z_collect(held))
        return jnp.concatenate(found, axis=0)


def body(
    tokens,
    cotangent,
    pair_table,
    doc_lengths,
    attn_gain,
    query_weight,
    key_matrix,
    value_matrix,
    output_weight,
    mlp_gain,
    gate_weight,
    up_weight,
    down_weight,
):
    low = jnp.bfloat16
    wide = jnp.float32
    ctx_count = lax.axis_size("c")
    wires = Wires(ctx_count)
    shard_length = tokens.shape[1]
    block_len = shard_length // 2
    length = shard_length * ctx_count
    c, x, k = wires.c, wires.x, wires.k
    heads = QUERY_HEADS // ctx_count
    head_width = heads * HEAD_SIZE
    share = max(1, ctx_count // KEY_VALUE_HEADS)
    kv_index = c // share
    kv_part = HEAD_SIZE // share
    hidden_total = gate_weight.shape[1]
    hidden_chip = hidden_total // (2 * ctx_count)
    score_scale = 1.0 / math.sqrt(HEAD_SIZE)

    def mm(left, right):
        return jnp.dot(left, right, preferred_element_type=wide)

    def mm_t(left, right):
        return jnp.einsum("ij,kj->ik", left, right, preferred_element_type=wide)

    def t_mm(left, right):
        return jnp.einsum("ti,tj->ij", left, right, preferred_element_type=wide)

    places = layout_places(pair_table, block_len, length)
    docs, rot = document_places(places, doc_lengths[0])
    cosine_table, sine_table = rope_tables(rot, HEAD_SIZE // 2)

    own = tokens[0]
    own_wide = own.astype(wide)
    dy = cotangent[0]

    rows = wires.ctx_gather(own).reshape(length, MODEL_WIDTH)
    gains = wires.over_fsdp(jnp.stack([attn_gain, mlp_gain], axis=1)).astype(wide)
    attn_gain_f = gains[:, 0]
    mlp_gain_f = gains[:, 1]
    take = lambda array, start, size: lax.dynamic_slice_in_dim(array, start, size, axis=1)
    head_weights = wires.over_fsdp(
        jnp.concatenate(
            [
                take(query_weight, c * head_width, head_width),
                take(key_matrix, kv_index * HEAD_SIZE, HEAD_SIZE),
                take(value_matrix, kv_index * HEAD_SIZE, HEAD_SIZE),
            ],
            axis=1,
        )
    )
    output_full = wires.over_fsdp(output_weight)

    normed_one, _ = rms_forward(rows.astype(wide), attn_gain_f)
    normed_one = normed_one.astype(low)
    projected = mm(normed_one, head_weights)
    q_rot = apply_rotation(
        projected[:, :head_width].reshape(length, heads, HEAD_SIZE), cosine_table, sine_table
    ).astype(low)
    k_rot = apply_rotation(
        projected[:, None, head_width : head_width + HEAD_SIZE], cosine_table, sine_table
    ).astype(low)[:, 0]
    v_low = projected[:, head_width + HEAD_SIZE :].astype(low)
    allowed = (places[None, :] <= places[:, None]) & (docs[None, :] == docs[:, None])

    def scores_of(queries):
        raw = jnp.einsum("rhd,ld->hrl", queries, k_rot, preferred_element_type=wide) * score_scale
        return jnp.where(allowed[None], raw, masked_score)

    scores = scores_of(q_rot)
    row_max = jnp.max(scores, axis=2, keepdims=True)
    exponent = jnp.exp(scores - row_max)
    row_total = jnp.sum(exponent, axis=2, keepdims=True)
    probs = exponent / row_total
    probs_low = probs.astype(low)
    mixed = (
        jnp.einsum("hrl,ld->rhd", probs_low, v_low, preferred_element_type=wide)
        .astype(low)
        .reshape(length, head_width)
    )
    mixed_rows = lax.all_to_all(mixed, "c", 0, 1, tiled=True)
    hidden = own_wide + mm(mixed_rows, output_full)
    normed_two, scale_two = rms_forward(hidden, mlp_gain_f)
    normed_two = normed_two.astype(low)

    def chip_columns(weight):
        start = hidden_chip * 2 * c
        mine = take(weight, start + hidden_chip * x, hidden_chip)
        theirs = take(weight, start + hidden_chip * (1 - x), hidden_chip)
        other = wires.swap(theirs, 2)
        near = x == 0
        both = jnp.stack([jnp.where(near, mine, other), jnp.where(near, other, mine)])
        partner = wires.swap(both, 1)
        first = k == 0
        even = jnp.where(first, both, partner)
        odd = jnp.where(first, partner, both)
        return jnp.stack([even, odd], axis=1).reshape(MODEL_WIDTH, hidden_chip)

    gate_chip = chip_columns(gate_weight)
    up_chip = chip_columns(up_weight)
    down_shard = down_weight.shape[0]
    holder = (2 * hidden_chip * c) // down_shard
    inside = 2 * hidden_chip * c - holder * down_shard
    down_mine = lax.dynamic_slice_in_dim(down_weight, inside + hidden_chip * x, hidden_chip)
    down_theirs = lax.dynamic_slice_in_dim(down_weight, inside + hidden_chip * (1 - x), hidden_chip)
    crossing = []
    for place in range(ctx_count):
        source = (2 * hidden_chip * place) // down_shard
        crossing.append((place * 4 + source, place * 4 + (source ^ 2)))
    down_other = wires.send(down_theirs, crossing)
    down_held = jnp.where(holder // 2 == x, down_mine, down_other)
    down_chip = jnp.where(holder % 2 == k, down_held, wires.swap(down_held, 1))

    normed_all = wires.spread(normed_two)
    dy_all = wires.spread(dy)
    out_parts = []
    grad_parts = []
    gate_term = 0.0
    up_term = 0.0
    down_term = 0.0
    for normed_rows, dy_rows in zip(normed_all, dy_all):
        gate_proj = mm(normed_rows, gate_chip)
        up_proj = mm(normed_rows, up_chip)
        sigmoid_gate = jax.nn.sigmoid(gate_proj)
        silu_gate = gate_proj * sigmoid_gate
        activated = (silu_gate * up_proj).astype(low)
        grad_act = mm_t(dy_rows, down_chip)
        grad_up = (grad_act * silu_gate).astype(low)
        grad_gate = (
            grad_act * up_proj * sigmoid_gate * (1.0 + gate_proj * (1.0 - sigmoid_gate))
        ).astype(low)
        out_parts.append(mm(activated, down_chip))
        grad_parts.append(mm_t(grad_gate, gate_chip) + mm_t(grad_up, up_chip))
        gate_term = gate_term + t_mm(normed_rows, grad_gate)
        up_term = up_term + t_mm(normed_rows, grad_up)
        down_term = down_term + t_mm(activated, dy_rows)
    normed_term = wires.collect(grad_parts)
    branch = wires.collect(out_parts)
    output = (hidden + branch).astype(low).reshape(tokens.shape)

    def core_sum(parts, axis):
        mine = lax.dynamic_index_in_dim(parts, k, axis, keepdims=False)
        theirs = lax.dynamic_index_in_dim(parts, 1 - k, axis, keepdims=False)
        return mine + wires.swap(theirs, 1)

    down_out = core_sum(down_term.reshape(2, hidden_chip // 2, MODEL_WIDTH), 0)
    row_count = MODEL_WIDTH // (4 * ctx_count)

    def columns_out(term):
        parts = core_sum(term.reshape(2 * ctx_count, 2, row_count, hidden_chip), 1)
        moved = lax.all_to_all(parts.astype(low), CHIPS, 0, 0, tiled=True)
        return moved.transpose(1, 0, 2).reshape(row_count, hidden_total).astype(wide)

    gate_out = columns_out(gate_term)
    up_out = columns_out(up_term)

    grad_hidden_part, mlp_gain_grad = rms_backward(hidden, scale_two, mlp_gain_f, normed_term)
    grad_hidden = dy.astype(wide) + grad_hidden_part
    grad_branch = grad_hidden.astype(low)
    grad_mixed_rows = mm_t(grad_branch, output_full).astype(low)
    grad_mixed = lax.all_to_all(grad_mixed_rows, "c", 1, 0, tiled=True)
    branch_rows = wires.ctx_gather(grad_branch).reshape(length, MODEL_WIDTH)
    output_term = t_mm(mixed, branch_rows)
    output_out = wires.sum_fsdp(output_term.reshape(4, row_count, MODEL_WIDTH), 0)

    grad_heads = grad_mixed.reshape(length, heads, HEAD_SIZE)
    grad_probs = jnp.einsum("rhd,ld->hrl", grad_heads, v_low, preferred_element_type=wide)
    inner_sum = jnp.sum(probs * grad_probs, axis=2, keepdims=True)
    grad_scores = (probs * (grad_probs - inner_sum)).astype(low)
    grad_q_rot = (
        jnp.einsum("hrl,ld->rhd", grad_scores, k_rot, preferred_element_type=wide) * score_scale
    )
    grad_k_rot = (
        jnp.einsum("hrl,rhd->ld", grad_scores, q_rot, preferred_element_type=wide) * score_scale
    )
    grad_v = jnp.einsum("hrl,rhd->ld", probs_low, grad_heads, preferred_element_type=wide)
    if share > 1:
        groups = [
            [(base * share + i) for i in range(share)] for base in range(ctx_count // share)
        ]
        both = lax.all_gather(
            jnp.stack([grad_k_rot, grad_v]), "c", axis=0, axis_index_groups=groups
        )
        both = jnp.sum(both, axis=0)
        grad_k_rot, grad_v = both[0], both[1]
    query_grad = (
        inverse_rotation(grad_q_rot, cosine_table, sine_table)
        .astype(low)
        .reshape(length, head_width)
    )
    key_grad = inverse_rotation(grad_k_rot[:, None], cosine_table, sine_table).astype(low)[:, 0]
    value_grad = grad_v.astype(low)
    if share > 1:
        key_grad = take(key_grad, (c % share) * kv_part, kv_part)
        value_grad = take(value_grad, (c % share) * kv_part, kv_part)
    packed = jnp.concatenate([query_grad, key_grad, value_grad], axis=1)
    packed_width = head_width + 2 * kv_part

    def unpack(rows_in):
        grid = rows_in.reshape(rows_in.shape[0], ctx_count, packed_width)
        flat = lambda piece: piece.reshape(rows_in.shape[0], -1)
        return (
            flat(grid[:, :, :head_width]),
            flat(grid[:, :, head_width : head_width + kv_part]),
            flat(grid[:, :, head_width + kv_part :]),
        )

    own_grads = unpack(lax.all_to_all(packed, "c", 0, 1, tiled=True))
    query_full = wires.over_fsdp(query_weight)
    key_full = wires.over_fsdp(key_matrix)
    value_full = wires.over_fsdp(value_matrix)
    grad_normed_one = (
        mm_t(own_grads[0], query_full)
        + mm_t(own_grads[1], key_full)
        + mm_t(own_grads[2], value_full)
    )
    scale_one = lax.rsqrt(jnp.mean(own_wide * own_wide, axis=-1, keepdims=True) + epsilon)
    grad_input_part, attn_gain_grad = rms_backward(
        own_wide, scale_one, attn_gain_f, grad_normed_one
    )
    input_grad = (grad_hidden + grad_input_part).astype(low).reshape(tokens.shape)

    packed_term = t_mm(normed_one, packed).reshape(ctx_count, 4, row_count, packed_width)
    packed_term = wires.sum_fsdp(packed_term, 1)
    packed_term = lax.all_to_all(packed_term, "c", 0, 0, tiled=True)
    query_out, key_out, value_out = unpack(
        packed_term.transpose(1, 0, 2).reshape(row_count, ctx_count * packed_width)
    )

    gain_parts = jnp.stack([attn_gain_grad, mlp_gain_grad]).reshape(2, 4 * ctx_count, row_count)
    gain_parts = lax.all_to_all(gain_parts.transpose(1, 0, 2), EVERY, 0, 0, tiled=True)
    gain_out = jnp.sum(gain_parts, axis=0)
    return (
        output,
        input_grad,
        gain_out[0],
        query_out,
        key_out,
        value_out,
        output_out,
        gain_out[1],
        gate_out,
        up_out,
        down_out,
    )


def solution(mesh):
    fsdp = ("x", "k")
    spread_all = ("c", "x", "k")
    ctx_count = mesh.shape["ctx"]
    grid = Mesh(mesh.devices.reshape(ctx_count, 2, 2), ("c", "x", "k"))
    row = P(fsdp, None)
    out_row = P(spread_all, None)
    act = P(fsdp, "c", None)
    return jax.shard_map(
        body,
        mesh=grid,
        in_specs=(act, act, P(), row, P(fsdp), row, row, row, row, P(fsdp), row, row, row),
        out_specs=(
            act,
            act,
            P(spread_all),
            out_row,
            out_row,
            out_row,
            out_row,
            P(spread_all),
            out_row,
            out_row,
            out_row,
        ),
        check_vma=False,
    )
```

```python
import math

import jax
import jax.numpy as jnp
from jax import lax
from jax.sharding import Mesh
from jax.sharding import PartitionSpec as P

MODEL_WIDTH = 2048
QUERY_HEADS = 32
KEY_VALUE_HEADS = 8
HEAD_SIZE = 64


epsilon = 1e-05
masked_score = -1e30


def rms_forward(values_in, norm_gain):
    scale_row = lax.rsqrt(jnp.mean(values_in * values_in, axis=-1, keepdims=True) + epsilon)
    return (values_in * scale_row * norm_gain, scale_row)


def rms_backward(values_in, scale_row, norm_gain, grad_normed):
    weighted = grad_normed * norm_gain
    inner_sum = jnp.mean(weighted * values_in, axis=-1, keepdims=True)
    grad_values = scale_row * weighted - values_in * scale_row * scale_row * scale_row * inner_sum
    grad_gain = jnp.sum(grad_normed * values_in * scale_row, axis=0)
    return (grad_values, grad_gain)


def rope_tables(rot_places, half_dim):
    frequency = 1.0 / 500000.0 ** (jnp.arange(half_dim, dtype=jnp.float32) * 2.0 / (2 * half_dim))
    angles = rot_places.astype(jnp.float32)[..., None] * frequency
    return (jnp.cos(angles), jnp.sin(angles))


def apply_rotation(vectors, cosine_table, sine_table):
    half_dim = vectors.shape[-1] // 2
    front_half = vectors[..., :half_dim]
    back_half = vectors[..., half_dim:]
    cos_heads = cosine_table[..., None, :]
    sin_heads = sine_table[..., None, :]
    return jnp.concatenate(
        [
            front_half * cos_heads - back_half * sin_heads,
            back_half * cos_heads + front_half * sin_heads,
        ],
        axis=-1,
    )


def inverse_rotation(vectors, cosine_table, sine_table):
    half_dim = vectors.shape[-1] // 2
    front_half = vectors[..., :half_dim]
    back_half = vectors[..., half_dim:]
    cos_heads = cosine_table[..., None, :]
    sin_heads = sine_table[..., None, :]
    return jnp.concatenate(
        [
            front_half * cos_heads + back_half * sin_heads,
            back_half * cos_heads - front_half * sin_heads,
        ],
        axis=-1,
    )


def layout_places(pair_table, block_len, sequence_length):
    row_ids = jnp.arange(sequence_length, dtype=jnp.int32)
    shard_ids = row_ids // (2 * block_len)
    within = row_ids % (2 * block_len)
    num_devices = pair_table.shape[0]
    device_ids = jnp.arange(num_devices, dtype=jnp.int32)
    chosen = jnp.sum(
        jnp.where(shard_ids[:, None] == device_ids[None, :], pair_table[None, :], 0), axis=1
    )
    block_ids = jnp.where(within < block_len, chosen, 2 * num_devices - 1 - chosen)
    return block_ids * block_len + within % block_len


def document_places(places, lengths_row):
    doc_ends = jnp.cumsum(lengths_row)
    doc_starts = doc_ends - lengths_row
    doc_ids = jnp.sum((places[:, None] >= doc_ends[None, :]).astype(jnp.int32), axis=1)
    doc_numbers = jnp.arange(lengths_row.shape[0], dtype=jnp.int32)
    picked = jnp.sum(
        jnp.where(doc_ids[:, None] == doc_numbers[None, :], doc_starts[None, :], 0), axis=1
    )
    return (doc_ids, places - picked)


EVERY = ("c", "x", "k")
CHIPS = ("c", "x")


def tie(first, second):
    return lax.optimization_barrier((first, second))[1]


class Wires:
    def __init__(self, ctx_count):
        self.count = ctx_count
        self.total = ctx_count * 4
        self.paths = ctx_count == 8
        self.c = lax.axis_index("c")
        self.x = lax.axis_index("x")
        self.k = lax.axis_index("k")
        self.f = 2 * self.x + self.k
        if self.paths:
            z_of = lambda i: i >> 3
            middle = [i for i in range(32) if z_of(i) in (1, 2)]
            ends = [i for i in range(32) if z_of(i) in (0, 3)]
            self.mid = [(i, i ^ 24) for i in middle]
            self.outward = [(i, i ^ 8) for i in middle]
            self.inward = [(i, i ^ 8) for i in ends]
            z_index = self.c // 2
            self.inner = (z_index == 1) | (z_index == 2)

    def swap(self, value, bits):
        return lax.ppermute(value, EVERY, [(i, i ^ bits) for i in range(self.total)])

    def send(self, value, pairs):
        return lax.ppermute(value, EVERY, pairs)

    def over_fsdp(self, shard):
        other = self.swap(shard, 2)
        near = self.x == 0
        both = jnp.stack([jnp.where(near, shard, other), jnp.where(near, other, shard)])
        partner = self.swap(both, 1)
        first = self.k == 0
        even = jnp.where(first, both, partner)
        odd = jnp.where(first, partner, both)
        return jnp.stack([even, odd], axis=1).reshape((-1,) + shard.shape[1:])

    def sum_fsdp(self, parts, axis):
        grid = jnp.moveaxis(parts, axis, 0)
        grid = grid.reshape((2, 2) + grid.shape[1:])
        mine = lax.dynamic_index_in_dim(grid, self.k, 1, keepdims=False)
        theirs = lax.dynamic_index_in_dim(grid, 1 - self.k, 1, keepdims=False)
        pair_sum = mine + self.swap(theirs, 1)
        mine = lax.dynamic_index_in_dim(pair_sum, self.x, 0, keepdims=False)
        theirs = lax.dynamic_index_in_dim(pair_sum, 1 - self.x, 0, keepdims=False)
        return mine + self.swap(theirs, 2)

    def ctx_gather(self, value):
        return lax.all_gather(value, "c", axis=0, tiled=False)

    def ctx_slots(self, value):
        half = value.shape[0] // 2
        if not self.paths:
            found = self.ctx_gather(value)
            return [found[:, :half], found[:, half:]]
        upper = self.z_spread(value[:half])
        lower = jnp.stack([value[half:], self.swap(value[half:], 4)])
        lower = self.z_spread(lower).reshape(self.count, half, -1)
        upper = jnp.stack([upper, self.swap(upper, 4)], axis=1).reshape(self.count, half, -1)
        return [upper, lower]

    def reslot(self, value, axis):
        if not self.paths:
            return value
        shape = value.shape
        value = value.reshape(shape[:axis] + (2, 2, 2) + shape[axis + 1 :])
        for step in range(3):
            value = jnp.where((self.c >> (2 - step)) & 1 == 1, jnp.flip(value, axis + step), value)
        return value.reshape(shape)

    def z_spread(self, value):
        step = self.swap(value, 8)
        over = self.send(value, self.mid)
        over_step = self.send(step, self.mid)
        out = self.send(over, self.outward)
        out_step = self.send(over_step, self.outward)
        second = jnp.where(self.inner, over_step, out)
        third = jnp.where(self.inner, over, out_step)
        return jnp.stack([value, step, second, third])

    def z_collect(self, parts):
        own, near, far, across = parts[0], parts[1], parts[2], parts[3]
        low = jnp.bfloat16
        wide = jnp.float32
        got = self.send(jnp.stack([far, across]).astype(low), self.inward).astype(wide)
        across = across + got[0]
        far = far + got[1]
        got = self.send(jnp.stack([across, far]).astype(low), self.mid).astype(wide)
        own = own + got[0]
        near = near + got[1]
        return own + self.swap(near.astype(low), 8).astype(wide)

    def spread(self, value):
        if not self.paths:
            return [lax.all_gather(value, CHIPS, axis=0, tiled=True)]
        half = value.shape[0] // 2
        width = value.shape[1]
        found = []
        for rows, order in ((value[:half], (4, 2)), (value[half:], (2, 4))):
            held = self.z_spread(rows)
            for bits in order:
                held = jnp.stack([held, self.swap(held, bits)])
            found.append(held.reshape(16 * half, width))
        return found

    def spread_late(self, value):
        if not self.paths:
            return self.spread(value)
        half = value.shape[0] // 2
        width = value.shape[1]
        found = []
        for rows, order in ((value[:half], (3, 2, 0, 1, 4, 5)), (value[half:], (2, 3, 0, 1, 4, 5))):
            held = lax.all_gather(rows, CHIPS, axis=0, tiled=False)
            held = held.reshape(2, 2, 2, 2, half, width)
            bits = ((self.c >> 2) & 1, (self.c >> 1) & 1, self.c & 1, self.x)
            for step, bit in enumerate(bits):
                held = jnp.where(bit == 1, jnp.flip(held, step), held)
            found.append(held.transpose(order).reshape(16 * half, width))
        return found

    def collect(self, parts):
        if not self.paths:
            low = parts[0].astype(jnp.bfloat16)
            return lax.psum_scatter(low, CHIPS, scatter_dimension=0, tiled=True).astype(jnp.float32)
        found = []
        for part, order in zip(parts, ((2, 4), (4, 2))):
            half = part.shape[0] // 16
            held = part.reshape(2, 2, 4, half, part.shape[1])
            for bits in order:
                held = held[0] + self.swap(held[1].astype(jnp.bfloat16), bits).astype(jnp.float32)
            found.append(self.z_collect(held))
        return jnp.concatenate(found, axis=0)


def body(
    tokens,
    cotangent,
    pair_table,
    doc_lengths,
    attn_gain,
    query_weight,
    key_matrix,
    value_matrix,
    output_weight,
    mlp_gain,
    gate_weight,
    up_weight,
    down_weight,
):
    low = jnp.bfloat16
    wide = jnp.float32
    ctx_count = lax.axis_size("c")
    wires = Wires(ctx_count)
    shard_length = tokens.shape[1]
    block_len = shard_length // 2
    length = shard_length * ctx_count
    c, x, k = wires.c, wires.x, wires.k
    heads = QUERY_HEADS // ctx_count
    head_width = heads * HEAD_SIZE
    share = max(1, ctx_count // KEY_VALUE_HEADS)
    kv_index = c // share
    kv_part = HEAD_SIZE // share
    hidden_total = gate_weight.shape[1]
    hidden_chip = hidden_total // (2 * ctx_count)
    score_scale = 1.0 / math.sqrt(HEAD_SIZE)

    def mm(left, right):
        return jnp.dot(left, right, preferred_element_type=wide)

    def mm_t(left, right):
        return jnp.einsum("ij,kj->ik", left, right, preferred_element_type=wide)

    def t_mm(left, right):
        return jnp.einsum("ti,tj->ij", left, right, preferred_element_type=wide)

    places = layout_places(pair_table, block_len, length).reshape(ctx_count, 2, block_len)
    places = wires.reslot(places, 0).transpose(1, 0, 2).reshape(length)
    docs, rot = document_places(places, doc_lengths[0])
    cosine_table, sine_table = rope_tables(rot, HEAD_SIZE // 2)

    own = tokens[0]
    own_wide = own.astype(wide)
    dy = cotangent[0]

    row_slots = wires.ctx_slots(own)
    gains = wires.over_fsdp(jnp.stack([attn_gain, mlp_gain], axis=1)).astype(wide)
    attn_gain_f = gains[:, 0]
    mlp_gain_f = gains[:, 1]
    take = lambda array, start, size: lax.dynamic_slice_in_dim(array, start, size, axis=1)
    head_weights = wires.over_fsdp(
        jnp.concatenate(
            [
                take(query_weight, c * head_width, head_width),
                take(key_matrix, kv_index * HEAD_SIZE, HEAD_SIZE),
                take(value_matrix, kv_index * HEAD_SIZE, HEAD_SIZE),
            ],
            axis=1,
        )
    )
    output_full = wires.over_fsdp(output_weight)

    normed_one = jnp.concatenate(
        [
            rms_forward(half.reshape(-1, MODEL_WIDTH).astype(wide), attn_gain_f)[0].astype(low)
            for half in row_slots
        ]
    )

    def to_rows(value):
        value = wires.reslot(value.reshape(2, ctx_count, block_len, -1), 1)
        return value.transpose(1, 0, 2, 3).reshape(length, -1)

    def from_rows(value):
        value = value.reshape(ctx_count, 2, block_len, -1).transpose(1, 0, 2, 3)
        return wires.reslot(value, 1).reshape(length, -1)

    dy_all = wires.spread_late(tie(row_slots, dy))
    gate_weight, up_weight, down_weight = tie(
        head_weights, (gate_weight, up_weight, down_weight)
    )
    projected = mm(normed_one, head_weights)
    q_rot = apply_rotation(
        projected[:, :head_width].reshape(length, heads, HEAD_SIZE), cosine_table, sine_table
    ).astype(low)
    k_rot = apply_rotation(
        projected[:, None, head_width : head_width + HEAD_SIZE], cosine_table, sine_table
    ).astype(low)[:, 0]
    v_low = projected[:, head_width + HEAD_SIZE :].astype(low)
    allowed = (places[None, :] <= places[:, None]) & (docs[None, :] == docs[:, None])

    def scores_of(queries):
        raw = jnp.einsum("rhd,ld->hrl", queries, k_rot, preferred_element_type=wide) * score_scale
        return jnp.where(allowed[None], raw, masked_score)

    scores = scores_of(q_rot)
    row_max = jnp.max(scores, axis=2, keepdims=True)
    exponent = jnp.exp(scores - row_max)
    row_total = jnp.sum(exponent, axis=2, keepdims=True)
    probs = exponent / row_total
    probs_low = probs.astype(low)
    mixed = (
        jnp.einsum("hrl,ld->rhd", probs_low, v_low, preferred_element_type=wide)
        .astype(low)
        .reshape(length, head_width)
    )
    mixed = to_rows(mixed)
    mixed_rows = lax.all_to_all(mixed, "c", 0, 1, tiled=True)
    hidden = own_wide + mm(mixed_rows, output_full)
    normed_two, scale_two = rms_forward(hidden, mlp_gain_f)
    normed_two = normed_two.astype(low)

    def chip_columns(weight):
        start = hidden_chip * 2 * c
        mine = take(weight, start + hidden_chip * x, hidden_chip)
        theirs = take(weight, start + hidden_chip * (1 - x), hidden_chip)
        other = wires.swap(theirs, 2)
        near = x == 0
        both = jnp.stack([jnp.where(near, mine, other), jnp.where(near, other, mine)])
        partner = wires.swap(both, 1)
        first = k == 0
        even = jnp.where(first, both, partner)
        odd = jnp.where(first, partner, both)
        return jnp.stack([even, odd], axis=1).reshape(MODEL_WIDTH, hidden_chip)

    gate_chip = chip_columns(gate_weight)
    up_chip = chip_columns(up_weight)
    down_shard = down_weight.shape[0]
    holder = (2 * hidden_chip * c) // down_shard
    inside = 2 * hidden_chip * c - holder * down_shard
    down_mine = lax.dynamic_slice_in_dim(down_weight, inside + hidden_chip * x, hidden_chip)
    down_theirs = lax.dynamic_slice_in_dim(down_weight, inside + hidden_chip * (1 - x), hidden_chip)
    crossing = []
    for place in range(ctx_count):
        source = (2 * hidden_chip * place) // down_shard
        crossing.append((place * 4 + source, place * 4 + (source ^ 2)))
    down_other = wires.send(down_theirs, crossing)
    down_held = jnp.where(holder // 2 == x, down_mine, down_other)
    down_chip = jnp.where(holder % 2 == k, down_held, wires.swap(down_held, 1))

    normed_all = wires.spread(normed_two)
    kept = []
    grad_parts = []
    for normed_rows, dy_rows in zip(normed_all, dy_all):
        gate_proj = mm(normed_rows, gate_chip)
        up_proj = mm(normed_rows, up_chip)
        sigmoid_gate = jax.nn.sigmoid(gate_proj)
        silu_gate = gate_proj * sigmoid_gate
        activated = (silu_gate * up_proj).astype(low)
        grad_act = mm_t(dy_rows, down_chip)
        grad_up = (grad_act * silu_gate).astype(low)
        grad_gate = (
            grad_act * up_proj * sigmoid_gate * (1.0 + gate_proj * (1.0 - sigmoid_gate))
        ).astype(low)
        grad_parts.append(
            (mm_t(grad_gate, gate_chip) + mm_t(grad_up, up_chip)).astype(low)
        )
        kept.append((activated, grad_gate, grad_up))
    kept = tie(grad_parts, kept)
    out_parts = [mm(activated, down_chip).astype(low) for activated, _, _ in kept]
    kept = tie(out_parts, kept)
    gate_term = 0.0
    up_term = 0.0
    down_term = 0.0
    for normed_rows, dy_rows, (activated, grad_gate, grad_up) in zip(normed_all, dy_all, kept):
        gate_term = gate_term + t_mm(normed_rows, grad_gate)
        up_term = up_term + t_mm(normed_rows, grad_up)
        down_term = down_term + t_mm(activated, dy_rows)
    normed_term = wires.collect(grad_parts)
    branch = wires.collect(tie(normed_term, out_parts))
    output = (hidden + branch).astype(low).reshape(tokens.shape)

    def core_sum(parts, axis):
        mine = lax.dynamic_index_in_dim(parts, k, axis, keepdims=False)
        theirs = lax.dynamic_index_in_dim(parts, 1 - k, axis, keepdims=False)
        return mine + wires.swap(theirs, 1)

    down_out = core_sum(down_term.reshape(2, hidden_chip // 2, MODEL_WIDTH), 0)
    row_count = MODEL_WIDTH // (4 * ctx_count)

    def columns_out(term):
        parts = core_sum(term.reshape(2 * ctx_count, 2, row_count, hidden_chip), 1)
        moved = lax.all_to_all(parts.astype(low), CHIPS, 0, 0, tiled=True)
        return moved.transpose(1, 0, 2).reshape(row_count, hidden_total).astype(wide)

    gate_out = columns_out(gate_term)
    up_out = columns_out(up_term)

    grad_hidden_part, mlp_gain_grad = rms_backward(hidden, scale_two, mlp_gain_f, normed_term)
    grad_hidden = dy.astype(wide) + grad_hidden_part
    grad_branch = grad_hidden.astype(low)
    grad_mixed_rows = mm_t(grad_branch, output_full).astype(low)
    grad_mixed = lax.all_to_all(grad_mixed_rows, "c", 1, 0, tiled=True)
    branch_rows = wires.ctx_gather(grad_branch).reshape(length, MODEL_WIDTH)
    output_term = t_mm(mixed, branch_rows)
    output_out = wires.sum_fsdp(output_term.reshape(4, row_count, MODEL_WIDTH), 0)

    grad_heads = from_rows(grad_mixed).reshape(length, heads, HEAD_SIZE)
    grad_probs = jnp.einsum("rhd,ld->hrl", grad_heads, v_low, preferred_element_type=wide)
    inner_sum = jnp.sum(probs * grad_probs, axis=2, keepdims=True)
    grad_scores = (probs * (grad_probs - inner_sum)).astype(low)
    grad_q_rot = (
        jnp.einsum("hrl,ld->rhd", grad_scores, k_rot, preferred_element_type=wide) * score_scale
    )
    grad_k_rot = (
        jnp.einsum("hrl,rhd->ld", grad_scores, q_rot, preferred_element_type=wide) * score_scale
    )
    grad_v = jnp.einsum("hrl,rhd->ld", probs_low, grad_heads, preferred_element_type=wide)
    if share > 1:
        groups = [
            [(base * share + i) for i in range(share)] for base in range(ctx_count // share)
        ]
        both = lax.all_gather(
            jnp.stack([grad_k_rot, grad_v]), "c", axis=0, axis_index_groups=groups
        )
        both = jnp.sum(both, axis=0)
        grad_k_rot, grad_v = both[0], both[1]
    query_grad = (
        inverse_rotation(grad_q_rot, cosine_table, sine_table)
        .astype(low)
        .reshape(length, head_width)
    )
    key_grad = inverse_rotation(grad_k_rot[:, None], cosine_table, sine_table).astype(low)[:, 0]
    value_grad = grad_v.astype(low)
    if share > 1:
        key_grad = take(key_grad, (c % share) * kv_part, kv_part)
        value_grad = take(value_grad, (c % share) * kv_part, kv_part)
    packed = jnp.concatenate([query_grad, key_grad, value_grad], axis=1)
    packed_width = head_width + 2 * kv_part

    def unpack(rows_in):
        grid = rows_in.reshape(rows_in.shape[0], ctx_count, packed_width)
        flat = lambda piece: piece.reshape(rows_in.shape[0], -1)
        return (
            flat(grid[:, :, :head_width]),
            flat(grid[:, :, head_width : head_width + kv_part]),
            flat(grid[:, :, head_width + kv_part :]),
        )

    own_grads = unpack(lax.all_to_all(to_rows(packed), "c", 0, 1, tiled=True))
    query_full = wires.over_fsdp(query_weight)
    key_full = wires.over_fsdp(key_matrix)
    value_full = wires.over_fsdp(value_matrix)
    grad_normed_one = (
        mm_t(own_grads[0], query_full)
        + mm_t(own_grads[1], key_full)
        + mm_t(own_grads[2], value_full)
    )
    scale_one = lax.rsqrt(jnp.mean(own_wide * own_wide, axis=-1, keepdims=True) + epsilon)
    grad_input_part, attn_gain_grad = rms_backward(
        own_wide, scale_one, attn_gain_f, grad_normed_one
    )
    input_grad = (grad_hidden + grad_input_part).astype(low).reshape(tokens.shape)

    packed_term = t_mm(normed_one, packed).reshape(ctx_count, 4, row_count, packed_width)
    packed_term = wires.sum_fsdp(packed_term, 1)
    packed_term = lax.all_to_all(packed_term, "c", 0, 0, tiled=True)
    query_out, key_out, value_out = unpack(
        packed_term.transpose(1, 0, 2).reshape(row_count, ctx_count * packed_width)
    )

    gain_parts = jnp.stack([attn_gain_grad, mlp_gain_grad]).reshape(2, 4 * ctx_count, row_count)
    gain_parts = lax.all_to_all(gain_parts.transpose(1, 0, 2), EVERY, 0, 0, tiled=True)
    gain_out = jnp.sum(gain_parts, axis=0)
    return (
        output,
        input_grad,
        gain_out[0],
        query_out,
        key_out,
        value_out,
        output_out,
        gain_out[1],
        gate_out,
        up_out,
        down_out,
    )


def solution(mesh):
    fsdp = ("x", "k")
    spread_all = ("c", "x", "k")
    ctx_count = mesh.shape["ctx"]
    grid = Mesh(mesh.devices.reshape(ctx_count, 2, 2), ("c", "x", "k"))
    row = P(fsdp, None)
    out_row = P(spread_all, None)
    act = P(fsdp, "c", None)
    return jax.shard_map(
        body,
        mesh=grid,
        in_specs=(act, act, P(), row, P(fsdp), row, row, row, row, P(fsdp), row, row, row),
        out_specs=(
            act,
            act,
            P(spread_all),
            out_row,
            out_row,
            out_row,
            out_row,
            P(spread_all),
            out_row,
            out_row,
            out_row,
        ),
        check_vma=False,
    )
```

```python
import math

import jax
import jax.numpy as jnp
from jax import lax
from jax.sharding import Mesh
from jax.sharding import PartitionSpec as P


MODEL_WIDTH = 2048
QUERY_HEADS = 32
KEY_VALUE_HEADS = 8
HEAD_SIZE = 64


epsilon = 1e-05
masked_score = -1e30


def rms_forward(values_in, norm_gain):
    scale_row = lax.rsqrt(jnp.mean(values_in * values_in, axis=-1, keepdims=True) + epsilon)
    return (values_in * scale_row * norm_gain, scale_row)


def rms_backward(values_in, scale_row, norm_gain, grad_normed):
    weighted = grad_normed * norm_gain
    inner_sum = jnp.mean(weighted * values_in, axis=-1, keepdims=True)
    grad_values = scale_row * weighted - values_in * scale_row * scale_row * scale_row * inner_sum
    grad_gain = jnp.sum(grad_normed * values_in * scale_row, axis=0)
    return (grad_values, grad_gain)


def rope_tables(rot_places, half_dim):
    frequency = 1.0 / 500000.0 ** (jnp.arange(half_dim, dtype=jnp.float32) * 2.0 / (2 * half_dim))
    angles = rot_places.astype(jnp.float32)[..., None] * frequency
    return (jnp.cos(angles), jnp.sin(angles))


def apply_rotation(vectors, cosine_table, sine_table):
    half_dim = vectors.shape[-1] // 2
    front_half = vectors[..., :half_dim]
    back_half = vectors[..., half_dim:]
    cos_heads = cosine_table[..., None, :]
    sin_heads = sine_table[..., None, :]
    return jnp.concatenate(
        [
            front_half * cos_heads - back_half * sin_heads,
            back_half * cos_heads + front_half * sin_heads,
        ],
        axis=-1,
    )


def inverse_rotation(vectors, cosine_table, sine_table):
    half_dim = vectors.shape[-1] // 2
    front_half = vectors[..., :half_dim]
    back_half = vectors[..., half_dim:]
    cos_heads = cosine_table[..., None, :]
    sin_heads = sine_table[..., None, :]
    return jnp.concatenate(
        [
            front_half * cos_heads + back_half * sin_heads,
            back_half * cos_heads - front_half * sin_heads,
        ],
        axis=-1,
    )


def layout_places(pair_table, block_len, sequence_length):
    row_ids = jnp.arange(sequence_length, dtype=jnp.int32)
    shard_ids = row_ids // (2 * block_len)
    within = row_ids % (2 * block_len)
    num_devices = pair_table.shape[0]
    device_ids = jnp.arange(num_devices, dtype=jnp.int32)
    chosen = jnp.sum(
        jnp.where(shard_ids[:, None] == device_ids[None, :], pair_table[None, :], 0), axis=1
    )
    block_ids = jnp.where(within < block_len, chosen, 2 * num_devices - 1 - chosen)
    return block_ids * block_len + within % block_len


def document_places(places, lengths_row):
    doc_ends = jnp.cumsum(lengths_row)
    doc_starts = doc_ends - lengths_row
    doc_ids = jnp.sum((places[:, None] >= doc_ends[None, :]).astype(jnp.int32), axis=1)
    doc_numbers = jnp.arange(lengths_row.shape[0], dtype=jnp.int32)
    picked = jnp.sum(
        jnp.where(doc_ids[:, None] == doc_numbers[None, :], doc_starts[None, :], 0), axis=1
    )
    return (doc_ids, places - picked)


EVERY = ("c", "x", "k")
CHIPS = ("c", "x")


class Wires:
    def __init__(self, ctx_count):
        self.count = ctx_count
        self.total = ctx_count * 4
        self.paths = ctx_count == 8
        self.c = lax.axis_index("c")
        self.x = lax.axis_index("x")
        self.k = lax.axis_index("k")
        if self.paths:
            z_of = lambda i: i >> 3
            middle = [i for i in range(32) if z_of(i) in (1, 2)]
            ends = [i for i in range(32) if z_of(i) in (0, 3)]
            self.mid = [(i, i ^ 24) for i in middle]
            self.outward = [(i, i ^ 8) for i in middle]
            self.inward = [(i, i ^ 8) for i in ends]
            z_index = self.c // 2
            self.inner = (z_index == 1) | (z_index == 2)

    def swap(self, value, bits):
        return lax.ppermute(value, EVERY, [(i, i ^ bits) for i in range(self.total)])

    def send(self, value, pairs):
        return lax.ppermute(value, EVERY, pairs)

    def over_fsdp(self, shard):
        other = self.swap(shard, 2)
        near = self.x == 0
        both = jnp.stack([jnp.where(near, shard, other), jnp.where(near, other, shard)])
        partner = self.swap(both, 1)
        first = self.k == 0
        even = jnp.where(first, both, partner)
        odd = jnp.where(first, partner, both)
        return jnp.stack([even, odd], axis=1).reshape((-1,) + shard.shape[1:])

    def fsdp_slots(self, shard):
        other = self.swap(shard, 2)
        return [shard, self.swap(shard, 1), other, self.swap(other, 1)]

    def fsdp_reslot(self, value):
        grid = value.reshape(value.shape[:-1] + (2, 2, value.shape[-1] // 4))
        axis = value.ndim - 1
        grid = jnp.where(self.x == 1, jnp.flip(grid, axis), grid)
        grid = jnp.where(self.k == 1, jnp.flip(grid, axis + 1), grid)
        return grid.reshape(value.shape)

    def sum_fsdp(self, parts, axis):
        grid = jnp.moveaxis(parts, axis, 0)
        grid = grid.reshape((2, 2) + grid.shape[1:])
        mine = lax.dynamic_index_in_dim(grid, self.k, 1, keepdims=False)
        theirs = lax.dynamic_index_in_dim(grid, 1 - self.k, 1, keepdims=False)
        pair_sum = mine + self.swap(theirs, 1)
        mine = lax.dynamic_index_in_dim(pair_sum, self.x, 0, keepdims=False)
        theirs = lax.dynamic_index_in_dim(pair_sum, 1 - self.x, 0, keepdims=False)
        return mine + self.swap(theirs, 2)

    def ctx_gather(self, value):
        return lax.all_gather(value, "c", axis=0, tiled=False)

    def ctx_slots(self, value):
        half = value.shape[0] // 2
        if not self.paths:
            found = self.ctx_gather(value)
            return [found[:, :half], found[:, half:]]
        upper = self.z_spread(value[:half])
        lower = jnp.stack([value[half:], self.swap(value[half:], 4)])
        lower = self.z_spread(lower).reshape(self.count, half, -1)
        upper = jnp.stack([upper, self.swap(upper, 4)], axis=1).reshape(self.count, half, -1)
        return [upper, lower]

    def reslot(self, value, axis):
        if not self.paths:
            return value
        shape = value.shape
        value = value.reshape(shape[:axis] + (2, 2, 2) + shape[axis + 1 :])
        for step in range(3):
            value = jnp.where((self.c >> (2 - step)) & 1 == 1, jnp.flip(value, axis + step), value)
        return value.reshape(shape)

    def z_spread(self, value):
        step = self.swap(value, 8)
        over = self.send(value, self.mid)
        over_step = self.send(step, self.mid)
        out = self.send(over, self.outward)
        out_step = self.send(over_step, self.outward)
        second = jnp.where(self.inner, over_step, out)
        third = jnp.where(self.inner, over, out_step)
        return jnp.stack([value, step, second, third])

    def z_collect(self, parts):
        own, near, far, across = parts[0], parts[1], parts[2], parts[3]
        low = jnp.bfloat16
        wide = jnp.float32
        got = self.send(jnp.stack([far, across]).astype(low), self.inward).astype(wide)
        across = across + got[0]
        far = far + got[1]
        got = self.send(jnp.stack([across, far]).astype(low), self.mid).astype(wide)
        own = own + got[0]
        near = near + got[1]
        return own + self.swap(near.astype(low), 8).astype(wide)

    def spread(self, value):
        if not self.paths:
            return [lax.all_gather(value, CHIPS, axis=0, tiled=True)]
        half = value.shape[0] // 2
        width = value.shape[1]
        found = []
        for rows, order in ((value[:half], (4, 2)), (value[half:], (2, 4))):
            held = self.z_spread(rows)
            for bits in order:
                held = jnp.stack([held, self.swap(held, bits)])
            found.append(held.reshape(16 * half, width))
        return found

    def spread_late(self, value):
        if not self.paths:
            return self.spread(value)
        half = value.shape[0] // 2
        width = value.shape[1]
        held = lax.all_gather(value, CHIPS, axis=0, tiled=False)
        held = held.reshape(2, 2, 2, 2, 2, half, width)
        bits = ((self.c >> 2) & 1, (self.c >> 1) & 1, self.c & 1, self.x)
        for step, bit in enumerate(bits):
            held = jnp.where(bit == 1, jnp.flip(held, step), held)
        return [
            held[:, :, :, :, part].transpose(order).reshape(16 * half, width)
            for part, order in enumerate(((3, 2, 0, 1, 4, 5), (2, 3, 0, 1, 4, 5)))
        ]

    def collect(self, parts):
        if not self.paths:
            low = parts[0].astype(jnp.bfloat16)
            return lax.psum_scatter(low, CHIPS, scatter_dimension=0, tiled=True).astype(jnp.float32)
        found = []
        for part, order in zip(parts, ((2, 4), (4, 2))):
            half = part.shape[0] // 16
            held = part.reshape(2, 2, 4, half, part.shape[1])
            for bits in order:
                held = held[0] + self.swap(held[1].astype(jnp.bfloat16), bits).astype(jnp.float32)
            found.append(self.z_collect(held))
        return jnp.concatenate(found, axis=0)


def body(
    tokens,
    cotangent,
    pair_table,
    doc_lengths,
    attn_gain,
    query_weight,
    key_matrix,
    value_matrix,
    output_weight,
    mlp_gain,
    gate_weight,
    up_weight,
    down_weight,
):
    low = jnp.bfloat16
    wide = jnp.float32
    ctx_count = lax.axis_size("c")
    wires = Wires(ctx_count)
    shard_length = tokens.shape[1]
    block_len = shard_length // 2
    length = shard_length * ctx_count
    c, x, k = wires.c, wires.x, wires.k
    heads = QUERY_HEADS // ctx_count
    head_width = heads * HEAD_SIZE
    share = max(1, ctx_count // KEY_VALUE_HEADS)
    kv_index = c // share
    kv_part = HEAD_SIZE // share
    hidden_total = gate_weight.shape[1]
    hidden_chip = hidden_total // (2 * ctx_count)
    score_scale = 1.0 / math.sqrt(HEAD_SIZE)

    def mm(left, right):
        return jnp.dot(left, right, preferred_element_type=wide)

    def mm_t(left, right):
        return jnp.einsum("ij,kj->ik", left, right, preferred_element_type=wide)

    def t_mm(left, right):
        return jnp.einsum("ti,tj->ij", left, right, preferred_element_type=wide)

    places = layout_places(pair_table, block_len, length).reshape(ctx_count, 2, block_len)
    places = wires.reslot(places, 0).transpose(1, 0, 2).reshape(length)
    docs, rot = document_places(places, doc_lengths[0])
    cosine_table, sine_table = rope_tables(rot, HEAD_SIZE // 2)

    own = tokens[0]
    own_wide = own.astype(wide)
    dy = cotangent[0]

    row_slots = wires.ctx_slots(own)
    gains = wires.over_fsdp(jnp.stack([attn_gain, mlp_gain], axis=1)).astype(wide)
    attn_gain_f = gains[:, 0]
    mlp_gain_f = gains[:, 1]
    take = lambda array, start, size: lax.dynamic_slice_in_dim(array, start, size, axis=1)
    head_shard = jnp.concatenate(
        [
            take(query_weight, c * head_width, head_width),
            take(key_matrix, kv_index * HEAD_SIZE, HEAD_SIZE),
            take(value_matrix, kv_index * HEAD_SIZE, HEAD_SIZE),
        ],
        axis=1,
    )
    head_weights = wires.over_fsdp(head_shard)
    output_slots = wires.fsdp_slots(output_weight)

    def parts_of(value):
        return jnp.split(value, 4, axis=-1)

    def from_slots(pieces):
        return wires.fsdp_reslot(jnp.concatenate(pieces, axis=-1))

    normed_one = jnp.concatenate(
        [
            rms_forward(half.reshape(-1, MODEL_WIDTH).astype(wide), attn_gain_f)[0].astype(low)
            for half in row_slots
        ]
    )

    def to_rows(value):
        value = wires.reslot(value.reshape(2, ctx_count, block_len, -1), 1)
        return value.transpose(1, 0, 2, 3).reshape(length, -1)

    def from_rows(value):
        value = value.reshape(ctx_count, 2, block_len, -1).transpose(1, 0, 2, 3)
        return wires.reslot(value, 1).reshape(length, -1)

    dy_all = wires.spread_late(dy)
    projected = mm(normed_one, head_weights)
    q_rot = apply_rotation(
        projected[:, :head_width].reshape(length, heads, HEAD_SIZE), cosine_table, sine_table
    ).astype(low)
    k_rot = apply_rotation(
        projected[:, None, head_width : head_width + HEAD_SIZE], cosine_table, sine_table
    ).astype(low)[:, 0]
    v_low = projected[:, head_width + HEAD_SIZE :].astype(low)
    allowed = (places[None, :] <= places[:, None]) & (docs[None, :] == docs[:, None])

    def scores_of(queries):
        raw = jnp.einsum("rhd,ld->hrl", queries, k_rot, preferred_element_type=wide) * score_scale
        return jnp.where(allowed[None], raw, masked_score)

    scores = scores_of(q_rot)
    row_max = jnp.max(scores, axis=2, keepdims=True)
    exponent = jnp.exp(scores - row_max)
    row_total = jnp.sum(exponent, axis=2, keepdims=True)
    probs = exponent / row_total
    probs_low = probs.astype(low)
    mixed = (
        jnp.einsum("hrl,ld->rhd", probs_low, v_low, preferred_element_type=wide)
        .astype(low)
        .reshape(length, head_width)
    )
    mixed = to_rows(mixed)
    mixed_rows = lax.all_to_all(mixed, "c", 0, 1, tiled=True)
    hidden = own_wide
    for piece, slot in zip(parts_of(wires.fsdp_reslot(mixed_rows)), output_slots):
        hidden = hidden + mm(piece, slot)
    normed_two, scale_two = rms_forward(hidden, mlp_gain_f)
    normed_two = normed_two.astype(low)

    def chip_columns(weight):
        start = hidden_chip * 2 * c
        mine = take(weight, start + hidden_chip * x, hidden_chip)
        theirs = take(weight, start + hidden_chip * (1 - x), hidden_chip)
        other = wires.swap(theirs, 2)
        near = x == 0
        both = jnp.stack([jnp.where(near, mine, other), jnp.where(near, other, mine)])
        partner = wires.swap(both, 1)
        first = k == 0
        even = jnp.where(first, both, partner)
        odd = jnp.where(first, partner, both)
        return jnp.stack([even, odd], axis=1).reshape(MODEL_WIDTH, hidden_chip)

    gate_chip = chip_columns(gate_weight)
    up_chip = chip_columns(up_weight)
    down_shard = down_weight.shape[0]
    holder = (2 * hidden_chip * c) // down_shard
    inside = 2 * hidden_chip * c - holder * down_shard
    down_mine = lax.dynamic_slice_in_dim(down_weight, inside + hidden_chip * x, hidden_chip)
    down_theirs = lax.dynamic_slice_in_dim(down_weight, inside + hidden_chip * (1 - x), hidden_chip)
    crossing = []
    for place in range(ctx_count):
        source = (2 * hidden_chip * place) // down_shard
        crossing.append((place * 4 + source, place * 4 + (source ^ 2)))
    down_other = wires.send(down_theirs, crossing)
    down_held = jnp.where(holder // 2 == x, down_mine, down_other)
    down_chip = jnp.where(holder % 2 == k, down_held, wires.swap(down_held, 1))

    normed_all = wires.spread(normed_two)
    kept = []
    grad_parts = []
    for normed_rows, dy_rows in zip(normed_all, dy_all):
        gate_proj = mm(normed_rows, gate_chip)
        up_proj = mm(normed_rows, up_chip)
        sigmoid_gate = jax.nn.sigmoid(gate_proj)
        silu_gate = gate_proj * sigmoid_gate
        activated = (silu_gate * up_proj).astype(low)
        grad_act = mm_t(dy_rows, down_chip)
        grad_up = (grad_act * silu_gate).astype(low)
        grad_gate = (
            grad_act * up_proj * sigmoid_gate * (1.0 + gate_proj * (1.0 - sigmoid_gate))
        ).astype(low)
        grad_parts.append(
            (mm_t(grad_gate, gate_chip) + mm_t(grad_up, up_chip)).astype(low)
        )
        kept.append((activated, grad_gate, grad_up))
    out_parts = [mm(activated, down_chip).astype(low) for activated, _, _ in kept]
    gate_term = 0.0
    up_term = 0.0
    down_term = 0.0
    for normed_rows, dy_rows, (activated, grad_gate, grad_up) in zip(normed_all, dy_all, kept):
        gate_term = gate_term + t_mm(normed_rows, grad_gate)
        up_term = up_term + t_mm(normed_rows, grad_up)
        down_term = down_term + t_mm(activated, dy_rows)
    normed_term = wires.collect(grad_parts)
    branch = wires.collect(out_parts)
    output = (hidden + branch).astype(low).reshape(tokens.shape)

    def core_sum(parts, axis):
        mine = lax.dynamic_index_in_dim(parts, k, axis, keepdims=False)
        theirs = lax.dynamic_index_in_dim(parts, 1 - k, axis, keepdims=False)
        return mine + wires.swap(theirs, 1)

    down_out = core_sum(down_term.reshape(2, hidden_chip // 2, MODEL_WIDTH), 0)
    row_count = MODEL_WIDTH // (4 * ctx_count)

    def columns_out(term):
        parts = core_sum(term.reshape(2 * ctx_count, 2, row_count, hidden_chip), 1)
        moved = lax.all_to_all(parts.astype(low), CHIPS, 0, 0, tiled=True)
        return moved.transpose(1, 0, 2).reshape(row_count, hidden_total).astype(wide)

    gate_out = columns_out(gate_term)
    up_out = columns_out(up_term)

    grad_hidden_part, mlp_gain_grad = rms_backward(hidden, scale_two, mlp_gain_f, normed_term)
    grad_hidden = dy.astype(wide) + grad_hidden_part
    grad_branch = grad_hidden.astype(low)
    grad_mixed_rows = from_slots([mm_t(grad_branch, slot).astype(low) for slot in output_slots])
    grad_mixed = lax.all_to_all(grad_mixed_rows, "c", 1, 0, tiled=True)
    branch_rows = wires.ctx_gather(grad_branch).reshape(length, MODEL_WIDTH)
    output_term = t_mm(mixed, branch_rows)
    output_out = wires.sum_fsdp(output_term.reshape(4, row_count, MODEL_WIDTH), 0)

    grad_heads = from_rows(grad_mixed).reshape(length, heads, HEAD_SIZE)
    grad_probs = jnp.einsum("rhd,ld->hrl", grad_heads, v_low, preferred_element_type=wide)
    inner_sum = jnp.sum(probs * grad_probs, axis=2, keepdims=True)
    grad_scores = (probs * (grad_probs - inner_sum)).astype(low)
    grad_q_rot = (
        jnp.einsum("hrl,ld->rhd", grad_scores, k_rot, preferred_element_type=wide) * score_scale
    )
    grad_k_rot = (
        jnp.einsum("hrl,rhd->ld", grad_scores, q_rot, preferred_element_type=wide) * score_scale
    )
    grad_v = jnp.einsum("hrl,rhd->ld", probs_low, grad_heads, preferred_element_type=wide)
    if share > 1:
        groups = [
            [(base * share + i) for i in range(share)] for base in range(ctx_count // share)
        ]
        both = lax.all_gather(
            jnp.stack([grad_k_rot, grad_v]), "c", axis=0, axis_index_groups=groups
        )
        both = jnp.sum(both, axis=0)
        grad_k_rot, grad_v = both[0], both[1]
    query_grad = (
        inverse_rotation(grad_q_rot, cosine_table, sine_table)
        .astype(low)
        .reshape(length, head_width)
    )
    key_grad = inverse_rotation(grad_k_rot[:, None], cosine_table, sine_table).astype(low)[:, 0]
    value_grad = grad_v.astype(low)
    if share > 1:
        key_grad = take(key_grad, (c % share) * kv_part, kv_part)
        value_grad = take(value_grad, (c % share) * kv_part, kv_part)
    packed = jnp.concatenate([query_grad, key_grad, value_grad], axis=1)
    packed_width = head_width + 2 * kv_part

    def unpack(rows_in):
        grid = rows_in.reshape(rows_in.shape[0], ctx_count, packed_width)
        flat = lambda piece: piece.reshape(rows_in.shape[0], -1)
        return (
            flat(grid[:, :, :head_width]),
            flat(grid[:, :, head_width : head_width + kv_part]),
            flat(grid[:, :, head_width + kv_part :]),
        )

    own_grads = unpack(lax.all_to_all(to_rows(packed), "c", 0, 1, tiled=True))
    late_slots = [wires.fsdp_slots(w) for w in (query_weight, key_matrix, value_matrix)]
    grad_normed_one = from_slots(
        [
            mm_t(own_grads[0], late_slots[0][slot])
            + mm_t(own_grads[1], late_slots[1][slot])
            + mm_t(own_grads[2], late_slots[2][slot])
            for slot in range(4)
        ]
    )
    scale_one = lax.rsqrt(jnp.mean(own_wide * own_wide, axis=-1, keepdims=True) + epsilon)
    grad_input_part, attn_gain_grad = rms_backward(
        own_wide, scale_one, attn_gain_f, grad_normed_one
    )
    input_grad = (grad_hidden + grad_input_part).astype(low).reshape(tokens.shape)

    packed_term = t_mm(normed_one, packed).reshape(ctx_count, 4, row_count, packed_width)
    packed_term = wires.sum_fsdp(packed_term, 1)
    packed_term = lax.all_to_all(packed_term, "c", 0, 0, tiled=True)
    query_out, key_out, value_out = unpack(
        packed_term.transpose(1, 0, 2).reshape(row_count, ctx_count * packed_width)
    )

    gain_parts = jnp.stack([attn_gain_grad, mlp_gain_grad]).reshape(2, 4 * ctx_count, row_count)
    gain_parts = lax.all_to_all(gain_parts.transpose(1, 0, 2), EVERY, 0, 0, tiled=True)
    gain_out = jnp.sum(gain_parts, axis=0)
    return (
        output,
        input_grad,
        gain_out[0],
        query_out,
        key_out,
        value_out,
        output_out,
        gain_out[1],
        gate_out,
        up_out,
        down_out,
    )


def solution(mesh):
    fsdp = ("x", "k")
    spread_all = ("c", "x", "k")
    ctx_count = mesh.shape["ctx"]
    grid = Mesh(mesh.devices.reshape(ctx_count, 2, 2), ("c", "x", "k"))
    row = P(fsdp, None)
    out_row = P(spread_all, None)
    act = P(fsdp, "c", None)
    return jax.shard_map(
        body,
        mesh=grid,
        in_specs=(act, act, P(), row, P(fsdp), row, row, row, row, P(fsdp), row, row, row),
        out_specs=(
            act,
            act,
            P(spread_all),
            out_row,
            out_row,
            out_row,
            out_row,
            P(spread_all),
            out_row,
            out_row,
            out_row,
        ),
        check_vma=False,
    )
```

```python
import math

import jax
import jax.numpy as jnp
from jax import lax
from jax.sharding import Mesh
from jax.sharding import PartitionSpec as P


MODEL_WIDTH = 2048
QUERY_HEADS = 32
KEY_VALUE_HEADS = 8
HEAD_SIZE = 64


epsilon = 1e-05
masked_score = -1e30


def rms_forward(values_in, norm_gain):
    scale_row = lax.rsqrt(jnp.mean(values_in * values_in, axis=-1, keepdims=True) + epsilon)
    return (values_in * scale_row * norm_gain, scale_row)


def rms_backward(values_in, scale_row, norm_gain, grad_normed):
    weighted = grad_normed * norm_gain
    inner_sum = jnp.mean(weighted * values_in, axis=-1, keepdims=True)
    grad_values = scale_row * weighted - values_in * scale_row * scale_row * scale_row * inner_sum
    grad_gain = jnp.sum(grad_normed * values_in * scale_row, axis=0)
    return (grad_values, grad_gain)


def rope_tables(rot_places, half_dim):
    frequency = 1.0 / 500000.0 ** (jnp.arange(half_dim, dtype=jnp.float32) * 2.0 / (2 * half_dim))
    angles = rot_places.astype(jnp.float32)[..., None] * frequency
    return (jnp.cos(angles), jnp.sin(angles))


def apply_rotation(vectors, cosine_table, sine_table):
    half_dim = vectors.shape[-1] // 2
    front_half = vectors[..., :half_dim]
    back_half = vectors[..., half_dim:]
    cos_heads = cosine_table[..., None, :]
    sin_heads = sine_table[..., None, :]
    return jnp.concatenate(
        [
            front_half * cos_heads - back_half * sin_heads,
            back_half * cos_heads + front_half * sin_heads,
        ],
        axis=-1,
    )


def inverse_rotation(vectors, cosine_table, sine_table):
    half_dim = vectors.shape[-1] // 2
    front_half = vectors[..., :half_dim]
    back_half = vectors[..., half_dim:]
    cos_heads = cosine_table[..., None, :]
    sin_heads = sine_table[..., None, :]
    return jnp.concatenate(
        [
            front_half * cos_heads + back_half * sin_heads,
            back_half * cos_heads - front_half * sin_heads,
        ],
        axis=-1,
    )


def layout_places(pair_table, block_len, sequence_length):
    row_ids = jnp.arange(sequence_length, dtype=jnp.int32)
    shard_ids = row_ids // (2 * block_len)
    within = row_ids % (2 * block_len)
    num_devices = pair_table.shape[0]
    device_ids = jnp.arange(num_devices, dtype=jnp.int32)
    chosen = jnp.sum(
        jnp.where(shard_ids[:, None] == device_ids[None, :], pair_table[None, :], 0), axis=1
    )
    block_ids = jnp.where(within < block_len, chosen, 2 * num_devices - 1 - chosen)
    return block_ids * block_len + within % block_len


def document_places(places, lengths_row):
    doc_ends = jnp.cumsum(lengths_row)
    doc_starts = doc_ends - lengths_row
    doc_ids = jnp.sum((places[:, None] >= doc_ends[None, :]).astype(jnp.int32), axis=1)
    doc_numbers = jnp.arange(lengths_row.shape[0], dtype=jnp.int32)
    picked = jnp.sum(
        jnp.where(doc_ids[:, None] == doc_numbers[None, :], doc_starts[None, :], 0), axis=1
    )
    return (doc_ids, places - picked)


EVERY = ("c", "x", "k")
CHIPS = ("c", "x")


class Wires:
    def __init__(self, ctx_count):
        self.count = ctx_count
        self.total = ctx_count * 4
        self.paths = ctx_count == 8
        self.c = lax.axis_index("c")
        self.x = lax.axis_index("x")
        self.k = lax.axis_index("k")
        if self.paths:
            z_of = lambda i: i >> 3
            middle = [i for i in range(32) if z_of(i) in (1, 2)]
            ends = [i for i in range(32) if z_of(i) in (0, 3)]
            self.mid = [(i, i ^ 24) for i in middle]
            self.outward = [(i, i ^ 8) for i in middle]
            self.inward = [(i, i ^ 8) for i in ends]
            z_index = self.c // 2
            self.inner = (z_index == 1) | (z_index == 2)

    def swap(self, value, bits):
        return lax.ppermute(value, EVERY, [(i, i ^ bits) for i in range(self.total)])

    def send(self, value, pairs):
        return lax.ppermute(value, EVERY, pairs)

    def over_fsdp(self, shard):
        other = self.swap(shard, 2)
        near = self.x == 0
        both = jnp.stack([jnp.where(near, shard, other), jnp.where(near, other, shard)])
        partner = self.swap(both, 1)
        first = self.k == 0
        even = jnp.where(first, both, partner)
        odd = jnp.where(first, partner, both)
        return jnp.stack([even, odd], axis=1).reshape((-1,) + shard.shape[1:])

    def fsdp_slots(self, shard):
        other = self.swap(shard, 2)
        return [shard, self.swap(shard, 1), other, self.swap(other, 1)]

    def fsdp_reslot(self, value):
        grid = value.reshape(value.shape[:-1] + (2, 2, value.shape[-1] // 4))
        axis = value.ndim - 1
        grid = jnp.where(self.x == 1, jnp.flip(grid, axis), grid)
        grid = jnp.where(self.k == 1, jnp.flip(grid, axis + 1), grid)
        return grid.reshape(value.shape)

    def sum_fsdp(self, parts, axis):
        grid = jnp.moveaxis(parts, axis, 0)
        grid = grid.reshape((2, 2) + grid.shape[1:])
        mine = lax.dynamic_index_in_dim(grid, self.k, 1, keepdims=False)
        theirs = lax.dynamic_index_in_dim(grid, 1 - self.k, 1, keepdims=False)
        pair_sum = mine + self.swap(theirs, 1)
        mine = lax.dynamic_index_in_dim(pair_sum, self.x, 0, keepdims=False)
        theirs = lax.dynamic_index_in_dim(pair_sum, 1 - self.x, 0, keepdims=False)
        return mine + self.swap(theirs, 2)

    def ctx_gather(self, value):
        return lax.all_gather(value, "c", axis=0, tiled=False)

    def ctx_slots(self, value):
        half = value.shape[0] // 2
        if not self.paths:
            found = self.ctx_gather(value)
            return [found[:, :half], found[:, half:]]
        upper = self.z_spread(value[:half])
        lower = jnp.stack([value[half:], self.swap(value[half:], 4)])
        lower = self.z_spread(lower).reshape(self.count, half, -1)
        upper = jnp.stack([upper, self.swap(upper, 4)], axis=1).reshape(self.count, half, -1)
        return [upper, lower]

    def reslot(self, value, axis):
        if not self.paths:
            return value
        shape = value.shape
        value = value.reshape(shape[:axis] + (2, 2, 2) + shape[axis + 1 :])
        for step in range(3):
            value = jnp.where((self.c >> (2 - step)) & 1 == 1, jnp.flip(value, axis + step), value)
        return value.reshape(shape)

    def z_spread(self, value):
        step = self.swap(value, 8)
        over = self.send(value, self.mid)
        over_step = self.send(step, self.mid)
        out = self.send(over, self.outward)
        out_step = self.send(over_step, self.outward)
        second = jnp.where(self.inner, over_step, out)
        third = jnp.where(self.inner, over, out_step)
        return jnp.stack([value, step, second, third])

    def z_collect(self, parts):
        own, near, far, across = parts[0], parts[1], parts[2], parts[3]
        low = jnp.bfloat16
        wide = jnp.float32
        got = self.send(jnp.stack([far, across]).astype(low), self.inward).astype(wide)
        across = across + got[0]
        far = far + got[1]
        got = self.send(jnp.stack([across, far]).astype(low), self.mid).astype(wide)
        own = own + got[0]
        near = near + got[1]
        return own + self.swap(near.astype(low), 8).astype(wide)

    def spread(self, value):
        if not self.paths:
            return [lax.all_gather(value, CHIPS, axis=0, tiled=True)]
        half = value.shape[0] // 2
        width = value.shape[1]
        found = []
        for rows, order in ((value[:half], (4, 2)), (value[half:], (2, 4))):
            held = self.z_spread(rows)
            for bits in order:
                held = jnp.stack([held, self.swap(held, bits)])
            found.append(held.reshape(16 * half, width))
        return found

    def spread_late(self, value):
        if not self.paths:
            return self.spread(value)
        half = value.shape[0] // 2
        width = value.shape[1]
        found = []
        for rows, order in ((value[:half], (3, 2, 0, 1, 4, 5)), (value[half:], (2, 3, 0, 1, 4, 5))):
            held = lax.all_gather(rows, CHIPS, axis=0, tiled=False)
            held = held.reshape(2, 2, 2, 2, half, width)
            bits = ((self.c >> 2) & 1, (self.c >> 1) & 1, self.c & 1, self.x)
            for step, bit in enumerate(bits):
                held = jnp.where(bit == 1, jnp.flip(held, step), held)
            found.append(held.transpose(order).reshape(16 * half, width))
        return found

    def collect(self, parts):
        if not self.paths:
            low = parts[0].astype(jnp.bfloat16)
            return lax.psum_scatter(low, CHIPS, scatter_dimension=0, tiled=True).astype(jnp.float32)
        found = []
        for part, order in zip(parts, ((2, 4), (4, 2))):
            half = part.shape[0] // 16
            held = part.reshape(2, 2, 4, half, part.shape[1])
            for bits in order:
                held = held[0] + self.swap(held[1].astype(jnp.bfloat16), bits).astype(jnp.float32)
            found.append(self.z_collect(held))
        return jnp.concatenate(found, axis=0)


def body(
    tokens,
    cotangent,
    pair_table,
    doc_lengths,
    attn_gain,
    query_weight,
    key_matrix,
    value_matrix,
    output_weight,
    mlp_gain,
    gate_weight,
    up_weight,
    down_weight,
):
    low = jnp.bfloat16
    wide = jnp.float32
    ctx_count = lax.axis_size("c")
    wires = Wires(ctx_count)
    shard_length = tokens.shape[1]
    block_len = shard_length // 2
    length = shard_length * ctx_count
    c, x, k = wires.c, wires.x, wires.k
    heads = QUERY_HEADS // ctx_count
    head_width = heads * HEAD_SIZE
    share = max(1, ctx_count // KEY_VALUE_HEADS)
    kv_index = c // share
    kv_part = HEAD_SIZE // share
    hidden_total = gate_weight.shape[1]
    hidden_chip = hidden_total // (2 * ctx_count)
    score_scale = 1.0 / math.sqrt(HEAD_SIZE)

    def mm(left, right):
        return jnp.dot(left, right, preferred_element_type=wide)

    def mm_t(left, right):
        return jnp.einsum("ij,kj->ik", left, right, preferred_element_type=wide)

    def t_mm(left, right):
        return jnp.einsum("ti,tj->ij", left, right, preferred_element_type=wide)

    places = layout_places(pair_table, block_len, length).reshape(ctx_count, 2, block_len)
    places = wires.reslot(places, 0).transpose(1, 0, 2).reshape(length)
    docs, rot = document_places(places, doc_lengths[0])
    cosine_table, sine_table = rope_tables(rot, HEAD_SIZE // 2)

    own = tokens[0]
    own_wide = own.astype(wide)
    dy = cotangent[0]

    row_slots = wires.ctx_slots(own)
    gains = wires.over_fsdp(jnp.stack([attn_gain, mlp_gain], axis=1)).astype(wide)
    attn_gain_f = gains[:, 0]
    mlp_gain_f = gains[:, 1]
    take = lambda array, start, size: lax.dynamic_slice_in_dim(array, start, size, axis=1)
    head_shard = jnp.concatenate(
        [
            take(query_weight, c * head_width, head_width),
            take(key_matrix, kv_index * HEAD_SIZE, HEAD_SIZE),
            take(value_matrix, kv_index * HEAD_SIZE, HEAD_SIZE),
        ],
        axis=1,
    )
    head_weights = wires.over_fsdp(head_shard)
    output_slots = wires.fsdp_slots(output_weight)

    def parts_of(value):
        return jnp.split(value, 4, axis=-1)

    def from_slots(pieces):
        return wires.fsdp_reslot(jnp.concatenate(pieces, axis=-1))

    normed_one = jnp.concatenate(
        [
            rms_forward(half.reshape(-1, MODEL_WIDTH).astype(wide), attn_gain_f)[0].astype(low)
            for half in row_slots
        ]
    )

    def to_rows(value):
        value = wires.reslot(value.reshape(2, ctx_count, block_len, -1), 1)
        return value.transpose(1, 0, 2, 3).reshape(length, -1)

    def from_rows(value):
        value = value.reshape(ctx_count, 2, block_len, -1).transpose(1, 0, 2, 3)
        return wires.reslot(value, 1).reshape(length, -1)

    dy_all = wires.spread_late(dy)
    projected = mm(normed_one, head_weights)
    q_rot = apply_rotation(
        projected[:, :head_width].reshape(length, heads, HEAD_SIZE), cosine_table, sine_table
    ).astype(low)
    k_rot = apply_rotation(
        projected[:, None, head_width : head_width + HEAD_SIZE], cosine_table, sine_table
    ).astype(low)[:, 0]
    v_low = projected[:, head_width + HEAD_SIZE :].astype(low)
    allowed = (places[None, :] <= places[:, None]) & (docs[None, :] == docs[:, None])

    def scores_of(queries):
        raw = jnp.einsum("rhd,ld->hrl", queries, k_rot, preferred_element_type=wide) * score_scale
        return jnp.where(allowed[None], raw, masked_score)

    scores = scores_of(q_rot)
    row_max = jnp.max(scores, axis=2, keepdims=True)
    exponent = jnp.exp(scores - row_max)
    row_total = jnp.sum(exponent, axis=2, keepdims=True)
    probs = exponent / row_total
    probs_low = probs.astype(low)
    mixed = (
        jnp.einsum("hrl,ld->rhd", probs_low, v_low, preferred_element_type=wide)
        .astype(low)
        .reshape(length, head_width)
    )
    mixed = to_rows(mixed)
    mixed_rows = lax.all_to_all(mixed, "c", 0, 1, tiled=True)
    hidden = own_wide
    for piece, slot in zip(parts_of(wires.fsdp_reslot(mixed_rows)), output_slots):
        hidden = hidden + mm(piece, slot)
    normed_two, scale_two = rms_forward(hidden, mlp_gain_f)
    normed_two = normed_two.astype(low)

    def chip_columns(weight):
        start = hidden_chip * 2 * c
        mine = take(weight, start + hidden_chip * x, hidden_chip)
        theirs = take(weight, start + hidden_chip * (1 - x), hidden_chip)
        other = wires.swap(theirs, 2)
        near = x == 0
        both = jnp.stack([jnp.where(near, mine, other), jnp.where(near, other, mine)])
        partner = wires.swap(both, 1)
        first = k == 0
        even = jnp.where(first, both, partner)
        odd = jnp.where(first, partner, both)
        return jnp.stack([even, odd], axis=1).reshape(MODEL_WIDTH, hidden_chip)

    gate_chip = chip_columns(gate_weight)
    up_chip = chip_columns(up_weight)
    down_shard = down_weight.shape[0]
    holder = (2 * hidden_chip * c) // down_shard
    inside = 2 * hidden_chip * c - holder * down_shard
    down_mine = lax.dynamic_slice_in_dim(down_weight, inside + hidden_chip * x, hidden_chip)
    down_theirs = lax.dynamic_slice_in_dim(down_weight, inside + hidden_chip * (1 - x), hidden_chip)
    crossing = []
    for place in range(ctx_count):
        source = (2 * hidden_chip * place) // down_shard
        crossing.append((place * 4 + source, place * 4 + (source ^ 2)))
    down_other = wires.send(down_theirs, crossing)
    down_held = jnp.where(holder // 2 == x, down_mine, down_other)
    down_chip = jnp.where(holder % 2 == k, down_held, wires.swap(down_held, 1))

    normed_all = wires.spread(normed_two)
    kept = []
    grad_parts = []
    for normed_rows, dy_rows in zip(normed_all, dy_all):
        gate_proj = mm(normed_rows, gate_chip)
        up_proj = mm(normed_rows, up_chip)
        sigmoid_gate = jax.nn.sigmoid(gate_proj)
        silu_gate = gate_proj * sigmoid_gate
        activated = (silu_gate * up_proj).astype(low)
        grad_act = mm_t(dy_rows, down_chip)
        grad_up = (grad_act * silu_gate).astype(low)
        grad_gate = (
            grad_act * up_proj * sigmoid_gate * (1.0 + gate_proj * (1.0 - sigmoid_gate))
        ).astype(low)
        grad_parts.append(
            (mm_t(grad_gate, gate_chip) + mm_t(grad_up, up_chip)).astype(low)
        )
        kept.append((activated, grad_gate, grad_up))
    out_parts = [mm(activated, down_chip).astype(low) for activated, _, _ in kept]
    gate_term = 0.0
    up_term = 0.0
    down_term = 0.0
    for normed_rows, dy_rows, (activated, grad_gate, grad_up) in zip(normed_all, dy_all, kept):
        gate_term = gate_term + t_mm(normed_rows, grad_gate)
        up_term = up_term + t_mm(normed_rows, grad_up)
        down_term = down_term + t_mm(activated, dy_rows)
    normed_term = wires.collect(grad_parts)
    branch = wires.collect(out_parts)
    output = (hidden + branch).astype(low).reshape(tokens.shape)

    def core_sum(parts, axis):
        mine = lax.dynamic_index_in_dim(parts, k, axis, keepdims=False)
        theirs = lax.dynamic_index_in_dim(parts, 1 - k, axis, keepdims=False)
        return mine + wires.swap(theirs, 1)

    down_out = core_sum(down_term.reshape(2, hidden_chip // 2, MODEL_WIDTH), 0)
    row_count = MODEL_WIDTH // (4 * ctx_count)

    def columns_out(term):
        parts = core_sum(term.reshape(2 * ctx_count, 2, row_count, hidden_chip), 1)
        moved = lax.all_to_all(parts.astype(low), CHIPS, 0, 0, tiled=True)
        return moved.transpose(1, 0, 2).reshape(row_count, hidden_total).astype(wide)

    gate_out = columns_out(gate_term)
    up_out = columns_out(up_term)

    grad_hidden_part, mlp_gain_grad = rms_backward(hidden, scale_two, mlp_gain_f, normed_term)
    grad_hidden = dy.astype(wide) + grad_hidden_part
    grad_branch = grad_hidden.astype(low)
    grad_mixed_rows = from_slots([mm_t(grad_branch, slot).astype(low) for slot in output_slots])
    grad_mixed = lax.all_to_all(grad_mixed_rows, "c", 1, 0, tiled=True)
    branch_rows = wires.ctx_gather(grad_branch).reshape(length, MODEL_WIDTH)
    output_term = t_mm(mixed, branch_rows)
    output_out = wires.sum_fsdp(output_term.reshape(4, row_count, MODEL_WIDTH), 0)

    grad_heads = from_rows(grad_mixed).reshape(length, heads, HEAD_SIZE)
    grad_probs = jnp.einsum("rhd,ld->hrl", grad_heads, v_low, preferred_element_type=wide)
    inner_sum = jnp.sum(probs * grad_probs, axis=2, keepdims=True)
    grad_scores = (probs * (grad_probs - inner_sum)).astype(low)
    grad_q_rot = (
        jnp.einsum("hrl,ld->rhd", grad_scores, k_rot, preferred_element_type=wide) * score_scale
    )
    grad_k_rot = (
        jnp.einsum("hrl,rhd->ld", grad_scores, q_rot, preferred_element_type=wide) * score_scale
    )
    grad_v = jnp.einsum("hrl,rhd->ld", probs_low, grad_heads, preferred_element_type=wide)
    if share > 1:
        groups = [
            [(base * share + i) for i in range(share)] for base in range(ctx_count // share)
        ]
        both = lax.all_gather(
            jnp.stack([grad_k_rot, grad_v]), "c", axis=0, axis_index_groups=groups
        )
        both = jnp.sum(both, axis=0)
        grad_k_rot, grad_v = both[0], both[1]
    query_grad = (
        inverse_rotation(grad_q_rot, cosine_table, sine_table)
        .astype(low)
        .reshape(length, head_width)
    )
    key_grad = inverse_rotation(grad_k_rot[:, None], cosine_table, sine_table).astype(low)[:, 0]
    value_grad = grad_v.astype(low)
    if share > 1:
        key_grad = take(key_grad, (c % share) * kv_part, kv_part)
        value_grad = take(value_grad, (c % share) * kv_part, kv_part)
    packed = jnp.concatenate([query_grad, key_grad, value_grad], axis=1)
    packed_width = head_width + 2 * kv_part

    def unpack(rows_in):
        grid = rows_in.reshape(rows_in.shape[0], ctx_count, packed_width)
        flat = lambda piece: piece.reshape(rows_in.shape[0], -1)
        return (
            flat(grid[:, :, :head_width]),
            flat(grid[:, :, head_width : head_width + kv_part]),
            flat(grid[:, :, head_width + kv_part :]),
        )

    own_grads = unpack(lax.all_to_all(to_rows(packed), "c", 0, 1, tiled=True))
    late_slots = [wires.fsdp_slots(w) for w in (query_weight, key_matrix, value_matrix)]
    grad_normed_one = from_slots(
        [
            mm_t(own_grads[0], late_slots[0][slot])
            + mm_t(own_grads[1], late_slots[1][slot])
            + mm_t(own_grads[2], late_slots[2][slot])
            for slot in range(4)
        ]
    )
    scale_one = lax.rsqrt(jnp.mean(own_wide * own_wide, axis=-1, keepdims=True) + epsilon)
    grad_input_part, attn_gain_grad = rms_backward(
        own_wide, scale_one, attn_gain_f, grad_normed_one
    )
    input_grad = (grad_hidden + grad_input_part).astype(low).reshape(tokens.shape)

    packed_term = t_mm(normed_one, packed).reshape(ctx_count, 4, row_count, packed_width)
    packed_term = wires.sum_fsdp(packed_term, 1)
    packed_term = lax.all_to_all(packed_term, "c", 0, 0, tiled=True)
    query_out, key_out, value_out = unpack(
        packed_term.transpose(1, 0, 2).reshape(row_count, ctx_count * packed_width)
    )

    gain_parts = jnp.stack([attn_gain_grad, mlp_gain_grad]).reshape(2, 4 * ctx_count, row_count)
    gain_parts = lax.all_to_all(gain_parts.transpose(1, 0, 2), EVERY, 0, 0, tiled=True)
    gain_out = jnp.sum(gain_parts, axis=0)
    return (
        output,
        input_grad,
        gain_out[0],
        query_out,
        key_out,
        value_out,
        output_out,
        gain_out[1],
        gate_out,
        up_out,
        down_out,
    )


def solution(mesh):
    fsdp = ("x", "k")
    spread_all = ("c", "x", "k")
    ctx_count = mesh.shape["ctx"]
    grid = Mesh(mesh.devices.reshape(ctx_count, 2, 2), ("c", "x", "k"))
    row = P(fsdp, None)
    out_row = P(spread_all, None)
    act = P(fsdp, "c", None)
    return jax.shard_map(
        body,
        mesh=grid,
        in_specs=(act, act, P(), row, P(fsdp), row, row, row, row, P(fsdp), row, row, row),
        out_specs=(
            act,
            act,
            P(spread_all),
            out_row,
            out_row,
            out_row,
            out_row,
            P(spread_all),
            out_row,
            out_row,
            out_row,
        ),
        check_vma=False,
    )
```
